256 devices in a mesh: section: 16 (over y_hi, x, core), ray: 8 (over z), dp: 2 (over y_lo).
Axes of the slice: x: 4, y: 4 (y_hi: 2, y_lo: 2; y = y_hi * 2 + y_lo), z: 8, core: 2. Of those that a mesh axis runs over, the one named last changes fastest.
Arguments:
- section_tokens: bfloat16 [16, 2, 1024, 1024], P('section', 'dp', 'ray'), may hold values from -6 to 6
- enc_ln1: float32 [16, 1024], P('section'), may hold values from 0.5 to 1.5
- enc_qkv: bfloat16 [16, 1024, 3, 1024], P('section', None, None, 'ray'), may hold values from -40 to 40
- enc_out: bfloat16 [16, 1024, 1024], P('section', 'ray'), may hold values from -0.1875 to 0.1875
- enc_ln2: float32 [16, 1024], P('section'), may hold values from 0.5 to 1.5
- enc_up: bfloat16 [16, 1024, 4096], P('section', None, 'ray'), may hold values from -0.1875 to 0.1875
- enc_down: bfloat16 [16, 4096, 1024], P('section', 'ray'), may hold values from -0.09375 to 0.09375
- set_latent: bfloat16 [2, 1024, 1024], P('dp', 'ray'), may hold values from -6 to 6
- ray_queries: bfloat16 [2, 32768, 1024], P('dp', ('section', 'ray')), may hold values from -6 to 6
- dec_query: bfloat16 [1024, 1024], P('section'), may hold values from -40 to 40
- dec_kv: bfloat16 [1024, 2, 1024], P('section'), may hold values from -1 to 1
- dec_out: bfloat16 [1024, 1024], P('section'), may hold values from -0.1875 to 0.1875
- feature_grad: bfloat16 [2, 32768, 1024], P('dp', ('section', 'ray')), may hold values from -2 to 2
Outputs:
- handed: bfloat16 [16, 2, 1024, 1024], P('section', 'dp', 'ray')
- finished: bfloat16 [2, 1024, 1024], P('dp', 'ray', 'section')
- ray_features: bfloat16 [2, 32768, 1024], P('dp', ('section', 'ray'))
- latent_grad: bfloat16 [2, 1024, 1024], P('dp', 'ray')
- out_grad: float32 [1024, 1024], replicated
The draws below stay inside these ranges and needn't reach their ends.
All inputs are finite; a program needn't handle non-finite values.
Results may differ from the reference program's by a relative error of at most 0.022.
The reference program's roundings to bfloat16 on the way count: a program that leaves them out, or rounds other values in their place, can miss the bound.
Values may be sent and summed in bfloat16 or wider, within the bound.
No kernel may reach another device: no remote copies, remote signals or barrier semaphores. Data moves between devices by JAX's collectives and lax.ppermute only.
A program may use at most 128 MiB of HBM per device.

```python
import math
import jax
import jax.numpy as jnp
from jax import lax

D = 1024
HEADS = 16
FF = 4096
RAY_DEV = 256
SECTIONS = 16
SCENES = 2
SCENE_TOK = 1024
RAYS = 32768
N_RAY = 8


def draw_enc_qkv(key, part):
    base = jnp.clip(jax.random.normal(key, (SECTIONS, D, 3, D), jnp.float32), -6.0, 6.0) / math.sqrt(D)
    return base.astype(jnp.bfloat16)


def scene_pair(key):
    latent = jnp.clip(jax.random.normal(jax.random.fold_in(key, 21), (SCENES, SCENE_TOK, D), jnp.float32), -6.0, 6.0)
    queries = jnp.clip(jax.random.normal(jax.random.fold_in(key, 22), (SCENES, RAYS, D), jnp.float32), -6.0, 6.0)
    return (latent.astype(jnp.bfloat16), queries.astype(jnp.bfloat16))


def draw_set_latent(key, part):
    return scene_pair(key)[0]


def draw_ray_queries(key, part):
    return scene_pair(key)[1]


def decoder_maps(key):
    pairs = jnp.clip(jax.random.normal(jax.random.fold_in(key, 31), (D, 2, D), jnp.float32), -6.0, 6.0) / math.sqrt(D)
    own = jnp.clip(jax.random.normal(jax.random.fold_in(key, 32), (D, D), jnp.float32), -6.0, 6.0) / math.sqrt(D)
    query = own
    return (query.astype(jnp.bfloat16), pairs.astype(jnp.bfloat16))


def draw_dec_query(key, part):
    return decoder_maps(key)[0]


def draw_dec_kv(key, part):
    return decoder_maps(key)[1]


def levels(key, shape, shards, least, top_value):
    def one(dim, blocks):
        draws = jax.random.uniform(jax.random.fold_in(jax.random.fold_in(key, 6), dim), (blocks,), jnp.float32, least / len(shards), top_value / len(shards))
        return jnp.repeat(jnp.exp(draws), shape[dim] // blocks).reshape((-1,) + (1,) * (len(shape) - dim - 1))

    loudness = one(*shards[0])
    for cut in shards[1:]:
        loudness = loudness * one(*cut)
    return loudness


def normal_values(key, dims, scale, bound, shards=(), kind=jnp.bfloat16):
    level = levels(key, dims, shards, -0.22, 0.18) if shards else 1.0
    entries = jax.random.normal(key, dims, jnp.float32) * scale * level
    return jnp.minimum(jnp.maximum(entries, -bound), bound).astype(kind)


def setup_inputs(seed: int = 0) -> dict:
    key_of = jax.random.split(jax.random.key(seed), 14)
    return {
        "section_tokens": normal_values(key_of[0], (SECTIONS, SCENES, SCENE_TOK, D), 1.0, 6.0, ((0, 16), (1, 2), (2, 8))),
        "enc_ln1": jnp.clip(1.0 + 0.1 * jax.random.normal(key_of[1], (SECTIONS, D), jnp.float32), 0.5, 1.5),
        "enc_qkv": draw_enc_qkv(jax.random.fold_in(key_of[13], 71), 0),
        "enc_out": normal_values(key_of[3], (SECTIONS, D, D), D ** -0.5, 0.1875, ((0, 16), (1, 8))),
        "enc_ln2": jnp.clip(1.0 + 0.1 * jax.random.normal(key_of[4], (SECTIONS, D), jnp.float32), 0.5, 1.5),
        "enc_up": normal_values(key_of[5], (SECTIONS, D, FF), D ** -0.5, 0.1875, ((0, 16), (2, 8))),
        "enc_down": normal_values(key_of[6], (SECTIONS, FF, D), FF ** -0.5, 0.09375, ((0, 16), (1, 8))),
        "set_latent": draw_set_latent(jax.random.fold_in(key_of[13], 71), 0),
        "ray_queries": draw_ray_queries(jax.random.fold_in(key_of[13], 71), 0),
        "dec_query": draw_dec_query(jax.random.fold_in(key_of[13], 71), 0),
        "dec_kv": draw_dec_kv(jax.random.fold_in(key_of[13], 71), 0),
        "dec_out": normal_values(key_of[11], (D, D), D ** -0.5, 0.1875, ((0, 16),)),
        "feature_grad": normal_values(key_of[12], (SCENES, RAYS, D), ((SCENE_TOK / (SCENES * RAYS)) ** 0.5), 2.0, ((0, 2), (1, 128))),
    }


def layer_norm(values, gain):
    values = values.astype(jnp.float32)
    center = values - lax.optimization_barrier(jnp.mean(values, -1, keepdims=True))
    spread = lax.optimization_barrier(jnp.mean(center * center, -1, keepdims=True))
    return center * lax.rsqrt(spread + 1e-05) * gain

def softmax_rows(scores):
    top = lax.optimization_barrier(jnp.max(scores, -1, keepdims=True))
    expo = jnp.exp(scores - top)
    return expo / lax.optimization_barrier(jnp.sum(expo, -1, keepdims=True))

def encoder_layer(tokens, gain_one, qkv_weight, out_weight, gain_two, up_weight, down_weight):
    length = tokens.shape[0]
    head_dim = D // HEADS
    group = D // N_RAY
    fgroup = FF // N_RAY
    normed = layer_norm(tokens, gain_one).astype(jnp.bfloat16)
    packed = jnp.dot(normed, qkv_weight.reshape(D, 3 * D), preferred_element_type=jnp.float32).astype(jnp.bfloat16)
    packed = packed.reshape(length, 3, HEADS, head_dim).astype(jnp.float32)
    scores = jnp.einsum('qhd,khd->hqk', packed[:, 0], packed[:, 1]) / math.sqrt(head_dim)
    probs = softmax_rows(scores).astype(jnp.bfloat16)
    mixed = jnp.einsum('hqk,khd->qhd', probs.astype(jnp.float32), packed[:, 2]).astype(jnp.bfloat16).reshape(length, D)
    parts = jnp.einsum('lrc,rcd->rld', mixed.reshape(length, N_RAY, group).astype(jnp.float32), out_weight.reshape(N_RAY, group, D).astype(jnp.float32))
    attn = lax.optimization_barrier(jnp.sum(lax.optimization_barrier(parts.astype(jnp.bfloat16)).astype(jnp.float32), 0))
    hidden = (tokens.astype(jnp.float32) + attn).astype(jnp.bfloat16)
    normed_two = layer_norm(hidden, gain_two).astype(jnp.bfloat16)
    upper = jax.nn.gelu(jnp.dot(normed_two, up_weight, preferred_element_type=jnp.float32), approximate=True).astype(jnp.bfloat16)
    parts_two = jnp.einsum('lrc,rcd->rld', upper.reshape(length, N_RAY, fgroup).astype(jnp.float32), down_weight.reshape(N_RAY, fgroup, D).astype(jnp.float32))
    down = lax.optimization_barrier(jnp.sum(lax.optimization_barrier(parts_two.astype(jnp.bfloat16)).astype(jnp.float32), 0))
    return (hidden.astype(jnp.float32) + down).astype(jnp.bfloat16)

def decoder_scene(latent, queries, cotangent, w_query, w_pairs, w_mix):
    head_dim = D // HEADS
    scale = 1.0 / math.sqrt(head_dim)
    length = latent.shape[0]
    pairs = jnp.dot(latent, w_pairs.reshape(D, 2 * D), preferred_element_type=jnp.float32).astype(jnp.bfloat16)
    keys = pairs[:, :D].reshape(length, HEADS, head_dim).astype(jnp.float32)
    values = pairs[:, D:].reshape(length, HEADS, head_dim).astype(jnp.float32)

    def block(carry, index):
        grad_mix, pair_sum = carry
        start = (index * RAY_DEV).astype(jnp.int32)
        rows = lax.dynamic_slice_in_dim(queries, start, RAY_DEV, 0)
        cot_rows = lax.dynamic_slice_in_dim(cotangent, start, RAY_DEV, 0)
        query = jnp.dot(rows, w_query, preferred_element_type=jnp.float32).astype(jnp.bfloat16).reshape(RAY_DEV, HEADS, head_dim).astype(jnp.float32)
        scores = jnp.einsum('rhd,lhd->hrl', query, keys) * scale
        probs = softmax_rows(scores)
        probs_low = probs.astype(jnp.bfloat16).astype(jnp.float32)
        attended = jnp.einsum('hrl,lhd->rhd', probs_low, values).astype(jnp.bfloat16).reshape(RAY_DEV, D)
        feats = (rows.astype(jnp.float32) + jnp.dot(attended, w_mix, preferred_element_type=jnp.float32)).astype(jnp.bfloat16)
        grad_mix = grad_mix + jnp.dot(attended.T, cot_rows, preferred_element_type=jnp.float32)
        attn_grad = jnp.dot(cot_rows, w_mix.T, preferred_element_type=jnp.float32).astype(jnp.bfloat16).reshape(RAY_DEV, HEADS, head_dim).astype(jnp.float32)
        prob_grad = jnp.einsum('rhd,lhd->hrl', attn_grad, values)
        delta = lax.optimization_barrier(jnp.sum(probs * prob_grad, -1, keepdims=True))
        score_grad = (probs * (prob_grad - delta) * scale).astype(jnp.bfloat16).astype(jnp.float32)
        key_grad = jnp.einsum('hrl,rhd->lhd', score_grad, query).reshape(length, D)
        value_grad = jnp.einsum('hrl,rhd->lhd', probs_low, attn_grad).reshape(length, D)
        part = jnp.stack([key_grad, value_grad], 1)
        pair_sum = pair_sum + lax.optimization_barrier(part.astype(jnp.bfloat16)).astype(jnp.float32)
        return ((grad_mix, pair_sum), feats)
    start_carry = (jnp.zeros((D, D), jnp.float32), jnp.zeros((length, 2, D), jnp.float32))
    (grad_mix, pair_sum), feats = lax.scan(block, start_carry, jnp.arange(RAYS // RAY_DEV, dtype=jnp.int32))
    feats = feats.reshape(RAYS, D)
    pair_low = pair_sum.astype(jnp.bfloat16)
    latent_grad = jnp.dot(pair_low[:, 0], w_pairs[:, 0, :].T, preferred_element_type=jnp.float32)
    latent_grad = latent_grad + jnp.dot(pair_low[:, 1], w_pairs[:, 1, :].T, preferred_element_type=jnp.float32)
    return (feats, latent_grad.astype(jnp.bfloat16), grad_mix)

def reference(section_tokens, enc_ln1, enc_qkv, enc_out, enc_ln2, enc_up, enc_down, set_latent, ray_queries, dec_query, dec_kv, dec_out, feature_grad):

    def section_step(inputs):
        tokens, gain_one, qkv_weight, out_weight, gain_two, up_weight, down_weight = inputs
        return jax.vmap(lambda scene: encoder_layer(scene, gain_one, qkv_weight, out_weight, gain_two, up_weight, down_weight))(tokens)
    outputs = lax.map(section_step, (section_tokens, enc_ln1, enc_qkv, enc_out, enc_ln2, enc_up, enc_down))
    handed = jnp.concatenate([jnp.zeros_like(outputs[:1]), outputs[:-1]], 0)
    finished = outputs[-1]
    features_all = []
    grads_all = []
    out_grad = jnp.zeros((D, D), jnp.float32)
    for scene in range(SCENES):
        feats, latent_grad, grad_mix = decoder_scene(set_latent[scene], ray_queries[scene], feature_grad[scene], dec_query, dec_kv, dec_out)
        features_all.append(feats)
        grads_all.append(latent_grad)
        out_grad = out_grad + grad_mix
    return (handed, finished, jnp.stack(features_all, 0), jnp.stack(grads_all, 0), out_grad)
```

```python
import math

import jax
import jax.numpy as jnp
from jax import lax
from jax.experimental import pallas as pl
from jax.experimental.pallas import tpu as pltpu
from jax.sharding import PartitionSpec as P

HEADS = 16


def shifted(value, axis, by):
    count = lax.axis_size(axis)
    pairs = [(i, i + by) for i in range(count) if 0 <= i + by < count]
    return lax.ppermute(value, axis, pairs)


def layer_norm(values, gain):
    values = values.astype(jnp.float32)
    center = values - jnp.mean(values, -1, keepdims=True)
    spread = jnp.mean(center * center, -1, keepdims=True)
    return center * lax.rsqrt(spread + 1e-05) * gain


def softmax_rows(scores):
    top = jnp.max(scores, -1, keepdims=True)
    expo = jnp.exp(scores - top)
    return expo / jnp.sum(expo, -1, keepdims=True)


def attend_heads(packed, head_dim):
    length = packed.shape[0]
    heads = packed.shape[1] // (3 * head_dim)
    split = packed.reshape(length, 3, heads, head_dim)
    scores = jnp.einsum(
        "qhd,khd->hqk", split[:, 0], split[:, 1], preferred_element_type=jnp.float32
    ) / math.sqrt(head_dim)
    probs = softmax_rows(scores).astype(jnp.bfloat16)
    mixed = jnp.einsum("hqk,khd->qhd", probs, split[:, 2], preferred_element_type=jnp.float32)
    return mixed.astype(jnp.bfloat16).reshape(length, heads * head_dim)


def exchange(blocks, axis):
    return lax.all_to_all(blocks, axis, split_axis=0, concat_axis=0, tiled=True)


def after(value, *others):
    return lax.optimization_barrier((value,) + others)[0]


def gather_small(value, axis):
    count = lax.axis_size(axis)
    return exchange(jnp.broadcast_to(value[None], (count,) + value.shape), axis)


NT = (((1,), (1,)), ((), ()))
TN = (((0,), (0,)), ((), ()))


def head_kernel(pairs_ref, rays_ref, mixed_ref, grads_ref, keys, values, values_t, key_sum, value_sum):
    step = pl.program_id(0)
    dim = keys.shape[1]
    scale = 1.0 / math.sqrt(dim)

    @pl.when(step == 0)
    def _():
        keys[...] = pairs_ref[:, :dim]
        values[...] = pairs_ref[:, dim:]
        values_t[...] = pairs_ref[:, dim:].T
        key_sum[...] = jnp.zeros_like(key_sum)
        value_sum[...] = jnp.zeros_like(value_sum)

    query = rays_ref[0, :dim, :]
    grad = rays_ref[0, dim:, :]
    scores = jnp.dot(keys[...], query, preferred_element_type=jnp.float32)
    top = jnp.max(scores, 0, keepdims=True)
    expo = jnp.exp((scores - top) * scale)
    probs = expo * (1.0 / jnp.sum(expo, 0, keepdims=True))
    low = probs.astype(jnp.bfloat16)
    mixed_ref[0] = jnp.dot(values_t[...], low, preferred_element_type=jnp.float32).astype(jnp.bfloat16)
    prob_grad = jnp.dot(values[...], grad, preferred_element_type=jnp.float32)
    delta = jnp.sum(probs * prob_grad, 0, keepdims=True)
    score_grad = (probs * (prob_grad - delta) * scale).astype(jnp.bfloat16)
    key_part = lax.dot_general(score_grad, query, NT, preferred_element_type=jnp.float32)
    value_part = lax.dot_general(low, grad, NT, preferred_element_type=jnp.float32)
    key_sum[...] += key_part.astype(jnp.bfloat16).astype(jnp.float32)
    value_sum[...] += value_part.astype(jnp.bfloat16).astype(jnp.float32)

    @pl.when(step == pl.num_programs(0) - 1)
    def _():
        grads_ref[:, :dim] = key_sum[...].astype(jnp.bfloat16)
        grads_ref[:, dim:] = value_sum[...].astype(jnp.bfloat16)


def attend_rays(pairs, rays):
    blocks, both, width = rays.shape
    length = pairs.shape[0]
    dim = both // 2
    work = blocks * width * length
    return pl.pallas_call(
        head_kernel,
        grid=(blocks,),
        in_specs=[
            pl.BlockSpec((length, both), lambda i: (0, 0)),
            pl.BlockSpec((1, both, width), lambda i: (i, 0, 0)),
        ],
        out_specs=[
            pl.BlockSpec((1, dim, width), lambda i: (i, 0, 0)),
            pl.BlockSpec((length, both), lambda i: (0, 0)),
        ],
        out_shape=[
            jax.ShapeDtypeStruct((blocks, dim, width), jnp.bfloat16),
            jax.ShapeDtypeStruct((length, both), jnp.bfloat16),
        ],
        scratch_shapes=[
            pltpu.VMEM((length, dim), jnp.bfloat16),
            pltpu.VMEM((length, dim), jnp.bfloat16),
            pltpu.VMEM((dim, length), jnp.bfloat16),
            pltpu.VMEM((length, dim), jnp.float32),
            pltpu.VMEM((length, dim), jnp.float32),
        ],
        compiler_params=pltpu.CompilerParams(dimension_semantics=("arbitrary",)),
        cost_estimate=pl.CostEstimate(
            flops=10 * work * dim, transcendentals=work, bytes_accessed=6 * blocks * dim * width
        ),
    )(pairs, rays)


def local(
    section_tokens,
    enc_ln1,
    enc_qkv,
    enc_out,
    enc_ln2,
    enc_up,
    enc_down,
    set_latent,
    ray_queries,
    dec_query,
    dec_kv,
    dec_out,
    feature_grad,
):
    tokens = section_tokens[0, 0]
    width = tokens.shape[1]
    head_dim = width // HEADS
    local_width = enc_out.shape[1]
    sections = lax.axis_size("section")
    rays = lax.axis_size("ray")
    latent = set_latent[0]
    queries = ray_queries[0]
    cotangent = feature_grad[0]
    f32, bf16 = jnp.float32, jnp.bfloat16

    share = dec_query.shape[0]
    both = jnp.concatenate([dec_query, dec_out], 1)
    w_both = lax.all_gather(both, "section", axis=0, tiled=True)
    w_query, w_mix = w_both[:, :width], w_both[:, width:]
    dec_kv = after(dec_kv, both)
    kv_rows = dec_kv.reshape(share, 2, HEADS, head_dim).transpose(0, 2, 1, 3)
    kv_rows = kv_rows.reshape(share, HEADS, 2 * head_dim)
    by_head = kv_rows.transpose(1, 0, 2)
    w_head = exchange(by_head, "section").reshape(width, 2 * head_dim)
    normed = layer_norm(after(tokens, by_head), enc_ln1[0]).astype(bf16)
    own_pairs = jnp.dot(after(latent, normed), w_head, preferred_element_type=f32).astype(bf16)
    pairs = gather_small(own_pairs, "ray").reshape(-1, 2 * head_dim)

    packed = jnp.dot(
        after(lax.all_gather(normed, "ray", axis=0, tiled=True), pairs),
        enc_qkv[0].reshape(width, 3 * local_width),
        preferred_element_type=f32,
    ).astype(bf16)
    mixed = attend_heads(packed, head_dim)
    attn_parts = jnp.dot(mixed, enc_out[0], preferred_element_type=f32).astype(bf16)
    attn_rows = lax.psum_scatter(attn_parts, "ray", scatter_dimension=0, tiled=True)

    queries = after(queries, attn_parts)
    query_t = lax.dot_general(w_query, queries, (((0,), (1,)), ((), ())), preferred_element_type=f32)
    grad_t = lax.dot_general(w_mix, cotangent, NT, preferred_element_type=f32)
    rows = queries.shape[0]
    packed_rays = jnp.concatenate(
        [
            query_t.astype(bf16).reshape(HEADS, head_dim, rows),
            grad_t.astype(bf16).reshape(HEADS, head_dim, rows),
        ],
        1,
    )
    attn_rows = after(attn_rows, packed_rays).astype(f32)
    hidden = (tokens.astype(f32) + attn_rows).astype(bf16)
    normed_two = layer_norm(hidden, enc_ln2[0]).astype(bf16)
    mixed_t, pair_grad = attend_rays(pairs, after(exchange(packed_rays, "section"), normed_two))
    attended_t = exchange(mixed_t, "section").reshape(width, rows)
    mix_term = jnp.dot(attended_t, cotangent, preferred_element_type=f32).astype(bf16)
    term = lax.psum_scatter(mix_term, "ray", scatter_dimension=0, tiled=True)
    upper = jax.nn.gelu(
        jnp.dot(
            after(lax.all_gather(normed_two, "ray", axis=0, tiled=True), mix_term),
            enc_up[0],
            preferred_element_type=f32,
        ),
        approximate=True,
    ).astype(bf16)
    lower_parts = jnp.dot(upper, enc_down[0], preferred_element_type=f32).astype(bf16)
    lower_rows = lax.psum_scatter(lower_parts, "ray", scatter_dimension=0, tiled=True).astype(f32)
    pair_grad, attended_t = lax.optimization_barrier((pair_grad, attended_t, lower_parts))[:2]
    features = (
        queries.astype(f32) + lax.dot_general(attended_t, w_mix, TN, preferred_element_type=f32)
    ).astype(bf16)

    count = latent.shape[0]
    pair_sum = jnp.sum(
        exchange(pair_grad.reshape(rays, count, 2 * head_dim), "ray").astype(f32), 0
    ).astype(bf16)
    latent_part = lax.dot_general(pair_sum, w_head, NT, preferred_element_type=f32).astype(bf16)
    latent_part = exchange(after(latent_part, features).reshape(sections, -1, width), "section")
    latent_rows = jnp.sum(latent_part.astype(f32), 0).astype(bf16)

    term = after(term, latent_rows)
    term = jnp.sum(exchange(term.reshape(sections, -1, width), "section").astype(f32), 0)
    term = term + lax.ppermute(term, "dp", [(0, 1), (1, 0)])
    term = gather_small(term.astype(bf16), "section").reshape(-1, width)
    out_grad = lax.all_gather(term, "ray", axis=0, tiled=True).astype(f32)
    latent_grad = gather_small(after(latent_rows, term), "section").reshape(count, width)

    layer_out = (hidden.astype(f32) + lower_rows).astype(bf16)
    handed = shifted(layer_out, "section", 1)
    columns = width // sections
    layer_out = after(layer_out, latent_grad)
    finished = exchange(layer_out.T.reshape(sections, columns, count), "section")[sections - 1].T
    return (handed[None, None], finished[None], features[None], latent_grad[None], out_grad)


def solution(mesh):
    return jax.shard_map(
        local,
        mesh=mesh,
        in_specs=(
            P("section", "dp", "ray", None),
            P("section", None),
            P("section", None, None, "ray"),
            P("section", "ray", None),
            P("section", None),
            P("section", None, "ray"),
            P("section", "ray", None),
            P("dp", "ray", None),
            P("dp", ("section", "ray"), None),
            P("section", None),
            P("section", None, None),
            P("section", None),
            P("dp", ("section", "ray"), None),
        ),
        out_specs=(
            P("section", "dp", "ray", None),
            P("dp", "ray", "section"),
            P("dp", ("section", "ray"), None),
            P("dp", "ray", None),
            P(),
        ),
        check_vma=False,
    )
```

```python
import functools
import math

import jax
import jax.numpy as jnp
from jax import lax
from jax.experimental import pallas as pl
from jax.experimental.pallas import tpu as pltpu
from jax.sharding import PartitionSpec as P

HEADS = 16


def layer_norm(values, gain):
    values = values.astype(jnp.float32)
    center = values - jnp.mean(values, -1, keepdims=True)
    spread = jnp.mean(center * center, -1, keepdims=True)
    return center * lax.rsqrt(spread + 1e-05) * gain


def softmax_rows(scores):
    top = jnp.max(scores, -1, keepdims=True)
    expo = jnp.exp(scores - top)
    return expo / jnp.sum(expo, -1, keepdims=True)


def attend_heads(packed, head_dim):
    length = packed.shape[0]
    heads = packed.shape[1] // (3 * head_dim)
    split = packed.reshape(length, 3, heads, head_dim)
    scores = jnp.einsum(
        "qhd,khd->hqk", split[:, 0], split[:, 1], preferred_element_type=jnp.float32
    ) / math.sqrt(head_dim)
    probs = softmax_rows(scores).astype(jnp.bfloat16)
    mixed = jnp.einsum("hqk,khd->qhd", probs, split[:, 2], preferred_element_type=jnp.float32)
    return mixed.astype(jnp.bfloat16).reshape(length, heads * head_dim)


NT = (((1,), (1,)), ((), ()))
TN = (((0,), (0,)), ((), ()))
CORES = 2
HIGH = 2


def turned(value, axis, by):
    count = lax.axis_size(axis)
    return lax.ppermute(value, axis, [(i, (i + by) % count) for i in range(count)])


def moved(value, high=0, along=0, core=0):
    count = lax.axis_size("section")
    line = count // (CORES * HIGH)
    pairs = []
    for source in range(count):
        c, x, y = source % CORES, source // CORES % line, source // (CORES * line)
        target = ((y ^ high) * line + (x + along) % line) * CORES + (c ^ core)
        pairs.append((source, target))
    return lax.ppermute(value, "section", pairs)


def exchange(blocks, axis):
    return lax.all_to_all(blocks, axis, split_axis=0, concat_axis=0, tiled=True)


def gather_small(value, axis):
    count = lax.axis_size(axis)
    return exchange(jnp.broadcast_to(value[None], (count,) + value.shape), axis)


def after(value, *others):
    return lax.optimization_barrier((value,) + others)[0]


def offsets(count):
    half = count // 2
    return [0] + [k for step in range(1, half) for k in (step, -step)] + [half]


def ring_gather(value, axis):
    count = lax.axis_size(axis)
    half = count // 2
    cut = value.shape[0] // 2
    found = {0: value}
    right, left = value, value
    for step in range(1, half):
        right, left = turned(right, axis, 1), turned(left, axis, -1)
        found[step], found[-step] = right, left
    upper, lower = turned(right[:cut], axis, 1), turned(left[cut:], axis, -1)
    found[half] = jnp.concatenate([upper, lower], 0)
    return found


def ring_scatter(blocks, axis):
    count = lax.axis_size(axis)
    half = count // 2
    cut = blocks[half].shape[1] // 2
    left = turned(blocks[half][:, :cut], axis, -1)
    right = turned(blocks[half][:, cut:], axis, 1)
    for step in range(half - 1, 0, -1):
        if step == half - 1:
            back, ahead = blocks[step], blocks[-step]
            left = jnp.concatenate([back[:, :cut] + left, back[:, cut:]], 1)
            right = jnp.concatenate([ahead[:, :cut], ahead[:, cut:] + right], 1)
        else:
            left, right = blocks[step] + left, blocks[-step] + right
        left, right = turned(left, axis, -1), turned(right, axis, 1)
    return blocks[0].astype(jnp.float32) + left.astype(jnp.float32) + right.astype(jnp.float32)


def rays_kernel(
    own_ref, other_ref, wq_ref, wo_ref, pairs_ref, sums_in, proj_in, mixed_ref, sums_ref, proj_ref, rays, query, grad, pairs_t
):
    block, head = pl.program_id(0), pl.program_id(1)
    dim = wq_ref.shape[0] // 2
    scale = 1.0 / math.sqrt(dim)

    @pl.when((block == 0) & (head == 0))
    def _():
        sums_ref[...] = sums_in[...]
        proj_ref[...] = proj_in[...]
        for i in range(2):
            pairs_t[i] = pairs_ref[:, 2 * dim * i : 2 * dim * (i + 1)].T

    @pl.when((block == 0) & (head == 0))
    def _():
        rays[...] = own_ref[...]

    @pl.when((block == 1) & (head == 0))
    def _():
        rays[...] = other_ref[...]

    @pl.when(head == 0)
    def _():
        both_query = lax.dot_general(wq_ref[...], rays[0], NT, preferred_element_type=jnp.float32)
        both_grad = lax.dot_general(wo_ref[...], rays[1], NT, preferred_element_type=jnp.float32)
        both_query, both_grad = both_query.astype(jnp.bfloat16), both_grad.astype(jnp.bfloat16)
        zero = jnp.zeros((dim, both_query.shape[1]), jnp.bfloat16)
        for i in range(2):
            query[i, :dim] = both_query[dim * i : dim * (i + 1)]
            query[i, dim:] = zero
            grad[i, :dim] = zero
            grad[i, dim:] = both_grad[dim * i : dim * (i + 1)]

    lanes = pl.ds(pl.multiple_of(2 * dim * head, 2 * dim), 2 * dim)
    pairs = pairs_ref[:, lanes]
    scores = jnp.dot(pairs, query[head], preferred_element_type=jnp.float32)
    top = jnp.max(scores, 0, keepdims=True)
    expo = jnp.exp((scores - top) * scale)
    probs = expo * (1.0 / jnp.sum(expo, 0, keepdims=True))
    low = probs.astype(jnp.bfloat16)
    mixed = jnp.dot(pairs_t[head, dim:], low, preferred_element_type=jnp.float32)
    mixed_ref[block, pl.ds(pl.multiple_of(dim * head, dim), dim), :] = mixed.astype(jnp.bfloat16)
    prob_grad = jnp.dot(pairs, grad[head], preferred_element_type=jnp.float32)
    delta = jnp.sum(probs * prob_grad, 0, keepdims=True)
    score_grad = (probs * (prob_grad - delta) * scale).astype(jnp.bfloat16)
    part = lax.dot_general(score_grad, query[head], NT, preferred_element_type=jnp.float32)
    part = part + lax.dot_general(low, grad[head], NT, preferred_element_type=jnp.float32)
    sums_ref[:, lanes] += part.astype(jnp.bfloat16).astype(jnp.float32)

    @pl.when(head == 1)
    def _():
        proj_ref[...] += jnp.dot(mixed_ref[block], rays[1], preferred_element_type=jnp.float32)


def attend_rays(own, other, wq, wo, pairs, sums, proj):
    _, width, model = own.shape
    length, columns = pairs.shape
    both = wq.shape[0]
    work = 4 * width * length

    def whole(shape):
        return pl.BlockSpec(shape, lambda i, j: (0,) * len(shape))

    return pl.pallas_call(
        rays_kernel,
        grid=(2, 2),
        in_specs=[whole(x.shape) for x in (own, other, wq, wo, pairs, sums, proj)],
        out_specs=[whole((2, both, width)), whole(sums.shape), whole(proj.shape)],
        out_shape=[
            jax.ShapeDtypeStruct((2, both, width), jnp.bfloat16),
            jax.ShapeDtypeStruct(sums.shape, jnp.float32),
            jax.ShapeDtypeStruct(proj.shape, jnp.float32),
        ],
        scratch_shapes=[
            pltpu.VMEM(own.shape, jnp.bfloat16),
            pltpu.VMEM((2, both, width), jnp.bfloat16),
            pltpu.VMEM((2, both, width), jnp.bfloat16),
            pltpu.VMEM((2, both, length), jnp.bfloat16),
        ],
        input_output_aliases={5: 1, 6: 2},
        compiler_params=pltpu.CompilerParams(dimension_semantics=("arbitrary", "arbitrary")),
        cost_estimate=pl.CostEstimate(
            flops=8 * both * work, transcendentals=work, bytes_accessed=8 * width * model
        ),
    )(own, other, wq, wo, pairs, sums, proj)


def place_kernel(where_ref, *refs):
    out_ref = refs[-1]
    for i, ref in enumerate(refs[:-1]):
        rows = ref.shape[0] // 2
        for j in range(2):
            out_ref[j, where_ref[i]] = ref[rows * j : rows * (j + 1)].astype(jnp.float32)


def placed(parts, where):
    rows, model = parts[0].shape
    return pl.pallas_call(
        place_kernel,
        grid_spec=pltpu.PrefetchScalarGridSpec(
            num_scalar_prefetch=1,
            grid=(1,),
            in_specs=[pl.BlockSpec((rows, model), lambda i, w: (0, 0)) for _ in parts],
            out_specs=pl.BlockSpec((2, len(parts), rows // 2, model), lambda i, w: (0, 0, 0, 0)),
        ),
        out_shape=jax.ShapeDtypeStruct((2, len(parts), rows // 2, model), jnp.float32),
    )(where, *parts)


def local(
    section_tokens,
    enc_ln1,
    enc_qkv,
    enc_out,
    enc_ln2,
    enc_up,
    enc_down,
    set_latent,
    ray_queries,
    dec_query,
    dec_kv,
    dec_out,
    feature_grad,
):
    tokens = section_tokens[0, 0]
    width = tokens.shape[1]
    head_dim = width // HEADS
    local_width = enc_out.shape[1]
    sections = lax.axis_size("section")
    count = lax.axis_size("ray")
    groups = sections // HIGH
    line = groups // CORES
    latent = set_latent[0]
    queries = ray_queries[0]
    cotangent = feature_grad[0]
    rows, share = tokens.shape[0], dec_query.shape[0]
    f32, bf16 = jnp.float32, jnp.bfloat16
    here = lax.axis_index("section")
    core, place, high = here % CORES, here // CORES % line, here // groups

    normed = layer_norm(tokens, enc_ln1[0]).astype(bf16)
    seen = ring_gather(normed, "ray")

    own = jnp.stack([queries, cotangent])
    ring = {0: own, 1: moved(own, along=1), -1: moved(own, along=-1)}
    ring[2] = jnp.stack([moved(ring[1][0], along=1), moved(ring[-1][1], along=-1)])
    partner = {k: moved(ring[k], core=1) for k in (0, 1, -1, 2)}

    q_cols = dec_query.reshape(share, HIGH, groups, head_dim).transpose(2, 0, 1, 3)
    kv_cols = dec_kv.reshape(share, 2, HIGH, groups, head_dim).transpose(3, 0, 2, 1, 4)
    cols = jnp.concatenate(
        [q_cols.reshape(groups, share, -1), kv_cols.reshape(groups, share, -1)], 2
    )
    cols = jnp.concatenate([cols] * HIGH, 0)
    w_heads = exchange(cols, "section").reshape(width, -1)
    wq = w_heads[:, : 2 * head_dim].T
    w_pairs = w_heads[:, 2 * head_dim :]
    far_rows = moved(dec_out, high=1)
    wo = jnp.where(
        high == 0,
        jnp.concatenate([dec_out, far_rows], 0),
        jnp.concatenate([far_rows, dec_out], 0),
    )
    own_pairs = jnp.dot(latent, w_pairs, preferred_element_type=f32).astype(bf16)
    pairs = gather_small(own_pairs, "ray").reshape(count * rows, -1)

    order = offsets(count)
    w_qkv = enc_qkv[0].reshape(width, 3 * local_width)
    packed = jnp.dot(
        jnp.concatenate([seen[k] for k in order], 0), w_qkv, preferred_element_type=f32
    ).astype(bf16)
    mixed = attend_heads(packed, head_dim)
    attn = jnp.dot(mixed, enc_out[0], preferred_element_type=f32).astype(bf16)
    attn = {k: attn[rows * i : rows * (i + 1)] for i, k in enumerate(order)}
    attn_rows = ring_scatter(attn, "ray")
    hidden = (tokens.astype(f32) + attn_rows).astype(bf16)
    normed_two = layer_norm(hidden, enc_ln2[0]).astype(bf16)
    seen_two = ring_gather(normed_two, "ray")

    sums = jnp.zeros((count * rows, 4 * head_dim), f32)
    proj = jnp.zeros((2 * head_dim, width), f32)
    back = {}
    for k in (0, 1, -1, 2):
        both_mixed, sums, proj = attend_rays(ring[k], partner[k], wq, wo, pairs, sums, proj)
        back[k, 0], back[k, 1] = both_mixed[0], both_mixed[1]

    lower = {}
    for step in range(count // 2 + 1):
        ks = [k for k in order if abs(k) == step]
        chunk = jnp.concatenate([seen_two[k] for k in ks], 0)
        upper = jax.nn.gelu(
            jnp.dot(chunk, enc_up[0], preferred_element_type=f32), approximate=True
        ).astype(bf16)
        part = jnp.dot(upper, enc_down[0], preferred_element_type=f32).astype(bf16)
        for i, k in enumerate(ks):
            lower[k] = part[rows * i : rows * (i + 1)]
    lower_rows = ring_scatter(lower, "ray")
    layer_out = (hidden.astype(f32) + lower_rows).astype(bf16)

    term = exchange(proj.astype(bf16).reshape(count, -1, width), "ray")
    term = jnp.sum(term.astype(f32), 0)
    term = term + moved(term, high=1)
    term = term + lax.ppermute(term, "dp", [(0, 1), (1, 0)])
    term = gather_small(term.astype(bf16), "ray").reshape(2 * head_dim, width)
    half = term.shape[0] // 2
    grads = {0: term, 1: moved(term, along=1), -1: moved(term, along=-1)}
    grads[2] = jnp.concatenate(
        [moved(grads[1][:half], along=1), moved(grads[-1][half:], along=-1)], 0
    )
    parts, where = [], []
    for k in (0, 1, -1, 2):
        for c in range(CORES):
            parts.append(moved(grads[k], core=1) if c else grads[k])
            where.append((place - k) % line * CORES + (core ^ c))
    out_grad = placed(parts, jnp.stack(where).astype(jnp.int32)).reshape(width, width)

    pair_sum = exchange(sums.astype(bf16).reshape(count, rows, -1), "ray")
    pair_sum = jnp.sum(pair_sum.astype(f32), 0).astype(bf16)
    latent_part = lax.dot_general(pair_sum, w_pairs, NT, preferred_element_type=f32).astype(bf16)
    latent_part = exchange(latent_part.reshape(sections, -1, width), "section")
    latent_rows = jnp.sum(latent_part.astype(f32), 0).astype(bf16)
    latent_grad = gather_small(latent_rows, "section").reshape(rows, width)

    wo_ring = {0: wo, 1: moved(wo, along=1), -1: moved(wo, along=-1), 2: moved(wo, along=2)}
    mixed_t, w_mix = [], []
    for k in (0, 1, -1, 2):
        for c in range(CORES):
            w_mix.append(moved(wo_ring[k], core=1) if c else wo_ring[k])
            source = back[-k if k != 2 else 2, c]
            mixed_t.append(moved(source, along=k, core=c) if k or c else source)
    features = (
        queries.astype(f32)
        + lax.dot_general(
            jnp.concatenate(mixed_t, 0), jnp.concatenate(w_mix, 0), TN, preferred_element_type=f32
        )
    ).astype(bf16)

    handed = lax.ppermute(layer_out, "section", [(i, i + 1) for i in range(sections - 1)])
    columns = width // sections
    finished = exchange(layer_out.T.reshape(sections, columns, rows), "section")[sections - 1].T
    return (handed[None, None], finished[None], features[None], latent_grad[None], out_grad)


def solution(mesh):
    return jax.shard_map(
        local,
        mesh=mesh,
        in_specs=(
            P("section", "dp", "ray", None),
            P("section", None),
            P("section", None, None, "ray"),
            P("section", "ray", None),
            P("section", None),
            P("section", None, "ray"),
            P("section", "ray", None),
            P("dp", "ray", None),
            P("dp", ("section", "ray"), None),
            P("section", None),
            P("section", None, None),
            P("section", None),
            P("dp", ("section", "ray"), None),
        ),
        out_specs=(
            P("section", "dp", "ray", None),
            P("dp", "ray", "section"),
            P("dp", ("section", "ray"), None),
            P("dp", "ray", None),
            P(),
        ),
        check_vma=False,
    )
```

```python
import functools
import math

import jax
import jax.numpy as jnp
from jax import lax
from jax.experimental import pallas as pl
from jax.experimental.pallas import tpu as pltpu
from jax.sharding import PartitionSpec as P

HEADS = 16


def layer_norm(values, gain):
    values = values.astype(jnp.float32)
    center = values - jnp.mean(values, -1, keepdims=True)
    spread = jnp.mean(center * center, -1, keepdims=True)
    return center * lax.rsqrt(spread + 1e-05) * gain


def softmax_rows(scores):
    top = jnp.max(scores, -1, keepdims=True)
    expo = jnp.exp(scores - top)
    return expo / jnp.sum(expo, -1, keepdims=True)


def attend_heads(packed, head_dim):
    length = packed.shape[0]
    heads = packed.shape[1] // (3 * head_dim)
    split = packed.reshape(length, 3, heads, head_dim)
    scores = jnp.einsum(
        "qhd,khd->hqk", split[:, 0], split[:, 1], preferred_element_type=jnp.float32
    ) / math.sqrt(head_dim)
    probs = softmax_rows(scores).astype(jnp.bfloat16)
    mixed = jnp.einsum("hqk,khd->qhd", probs, split[:, 2], preferred_element_type=jnp.float32)
    return mixed.astype(jnp.bfloat16).reshape(length, heads * head_dim)


NT = (((1,), (1,)), ((), ()))
TN = (((0,), (0,)), ((), ()))
CORES = 2
HIGH = 2


def moved(value, high=0, along=0, core=0):
    count = lax.axis_size("section")
    line = count // (CORES * HIGH)
    pairs = []
    for source in range(count):
        c, x, y = source % CORES, source // CORES % line, source // (CORES * line)
        target = ((y ^ high) * line + (x + along) % line) * CORES + (c ^ core)
        pairs.append((source, target))
    return lax.ppermute(value, "section", pairs)


def exchange(blocks, axis):
    return lax.all_to_all(blocks, axis, split_axis=0, concat_axis=0, tiled=True)


def gather_small(value, axis):
    count = lax.axis_size(axis)
    return exchange(jnp.broadcast_to(value[None], (count,) + value.shape), axis)


def after(value, *others):
    return lax.optimization_barrier((value,) + others)[0]


def rays_kernel(blocks, carried, *refs):
    ray_refs, (wq_ref, wo_ref, pairs_ref), refs = refs[:blocks], refs[blocks : blocks + 3], refs[blocks + 3 :]
    if carried:
        (sums_in, proj_in), refs = refs[:2], refs[2:]
    mixed_ref, sums_ref, proj_ref, rays, query, grad, pairs_t, sums, proj = refs
    block, head = pl.program_id(0), pl.program_id(1)
    dim = wq_ref.shape[0] // 2
    scale = 1.0 / math.sqrt(dim)

    @pl.when((block == 0) & (head == 0))
    def _():
        if carried:
            sums[...] = sums_in[...]
            proj[...] = proj_in[...]
        else:
            sums[...] = jnp.zeros_like(sums)
            proj[...] = jnp.zeros_like(proj)
        for i in range(2):
            pairs_t[i] = pairs_ref[:, 2 * dim * i : 2 * dim * (i + 1)].T

    for i in range(blocks):

        @pl.when((block == i) & (head == 0))
        def _(i=i):
            rays[...] = ray_refs[i][...]

    @pl.when(head == 0)
    def _():
        both_query = lax.dot_general(wq_ref[...], rays[0], NT, preferred_element_type=jnp.float32)
        both_grad = lax.dot_general(wo_ref[...], rays[1], NT, preferred_element_type=jnp.float32)
        both_query, both_grad = both_query.astype(jnp.bfloat16), both_grad.astype(jnp.bfloat16)
        zero = jnp.zeros((dim, both_query.shape[1]), jnp.bfloat16)
        for i in range(2):
            query[i, :dim] = both_query[dim * i : dim * (i + 1)]
            query[i, dim:] = zero
            grad[i, :dim] = zero
            grad[i, dim:] = both_grad[dim * i : dim * (i + 1)]

    lanes = pl.ds(pl.multiple_of(2 * dim * head, 2 * dim), 2 * dim)
    pairs = pairs_ref[:, lanes]
    scores = jnp.dot(pairs, query[head], preferred_element_type=jnp.float32)
    top = jnp.max(scores, 0, keepdims=True)
    expo = jnp.exp((scores - top) * scale)
    probs = expo * (1.0 / jnp.sum(expo, 0, keepdims=True))
    low = probs.astype(jnp.bfloat16)
    mixed = jnp.dot(pairs_t[head, dim:], low, preferred_element_type=jnp.float32)
    mixed_ref[block, pl.ds(pl.multiple_of(dim * head, dim), dim), :] = mixed.astype(jnp.bfloat16)
    prob_grad = jnp.dot(pairs, grad[head], preferred_element_type=jnp.float32)
    delta = jnp.sum(probs * prob_grad, 0, keepdims=True)
    score_grad = (probs * (prob_grad - delta) * scale).astype(jnp.bfloat16)
    part = lax.dot_general(score_grad, query[head], NT, preferred_element_type=jnp.float32)
    part = part + lax.dot_general(low, grad[head], NT, preferred_element_type=jnp.float32)
    sums[:, lanes] += part.astype(jnp.bfloat16).astype(jnp.float32)

    @pl.when(head == 1)
    def _():
        proj[...] += jnp.dot(mixed_ref[block], rays[1], preferred_element_type=jnp.float32)

    @pl.when((head == 1) & (block == blocks - 1))
    def _():
        sums_ref[...] = sums[...].astype(sums_ref.dtype)
        proj_ref[...] = proj[...].astype(proj_ref.dtype)


def attend_rays(rays, wq, wo, pairs, carry, kind):
    _, width, model = rays[0].shape
    length, columns = pairs.shape
    both, blocks = wq.shape[0], len(rays)
    work = 2 * blocks * width * length
    operands = [*rays, wq, wo, pairs, *carry]

    def whole(shape):
        return pl.BlockSpec(shape, lambda i, j: (0,) * len(shape))

    shapes = [(blocks, both, width), (length, columns), (both, model)]
    kinds = [jnp.bfloat16, kind, kind]
    return pl.pallas_call(
        functools.partial(rays_kernel, blocks, bool(carry)),
        grid=(blocks, 2),
        in_specs=[whole(x.shape) for x in operands],
        out_specs=[whole(x) for x in shapes],
        out_shape=[jax.ShapeDtypeStruct(x, k) for x, k in zip(shapes, kinds)],
        scratch_shapes=[
            pltpu.VMEM(rays[0].shape, jnp.bfloat16),
            pltpu.VMEM((2, both, width), jnp.bfloat16),
            pltpu.VMEM((2, both, width), jnp.bfloat16),
            pltpu.VMEM((2, both, length), jnp.bfloat16),
            pltpu.VMEM((length, columns), jnp.float32),
            pltpu.VMEM((both, model), jnp.float32),
        ],
        compiler_params=pltpu.CompilerParams(dimension_semantics=("arbitrary", "arbitrary")),
        cost_estimate=pl.CostEstimate(
            flops=8 * both * work, transcendentals=work, bytes_accessed=4 * blocks * width * model
        ),
    )(*operands)


def place_kernel(where_ref, *refs):
    out_ref = refs[-1]
    for i, ref in enumerate(refs[:-1]):
        steps, rows = ref.shape[0], ref.shape[1] // 2
        for k in range(steps):
            for j in range(2):
                out_ref[j, where_ref[steps * i + k]] = ref[k, rows * j : rows * (j + 1)].astype(jnp.float32)


def placed(parts, where):
    steps, rows, model = parts[0].shape
    out = (2, steps * len(parts), rows // 2, model)
    return pl.pallas_call(
        place_kernel,
        grid_spec=pltpu.PrefetchScalarGridSpec(
            num_scalar_prefetch=1,
            grid=(1,),
            in_specs=[pl.BlockSpec((steps, rows, model), lambda i, w: (0, 0, 0)) for _ in parts],
            out_specs=pl.BlockSpec(out, lambda i, w: (0, 0, 0, 0)),
        ),
        out_shape=jax.ShapeDtypeStruct(out, jnp.float32),
    )(where, *parts)


def local(
    section_tokens,
    enc_ln1,
    enc_qkv,
    enc_out,
    enc_ln2,
    enc_up,
    enc_down,
    set_latent,
    ray_queries,
    dec_query,
    dec_kv,
    dec_out,
    feature_grad,
):
    tokens = section_tokens[0, 0]
    width = tokens.shape[1]
    head_dim = width // HEADS
    local_width = enc_out.shape[1]
    sections = lax.axis_size("section")
    count = lax.axis_size("ray")
    groups = sections // HIGH
    line = groups // CORES
    latent = set_latent[0]
    queries = ray_queries[0]
    cotangent = feature_grad[0]
    rows, share = tokens.shape[0], dec_query.shape[0]
    f32, bf16 = jnp.float32, jnp.bfloat16
    here = lax.axis_index("section")
    core, place, high = here % CORES, here // CORES % line, here // groups

    normed = layer_norm(tokens, enc_ln1[0]).astype(bf16)
    seen = lax.all_gather(normed, "ray", axis=0, tiled=True)

    steps = (0, 1, -1, 2)
    own = jnp.stack([queries, cotangent])
    own = after(own, normed)
    ring = {0: own, 1: moved(own, along=1), -1: moved(own, along=-1)}
    partner = {0: moved(own, core=1)}

    q_cols = dec_query.reshape(share, HIGH, groups, head_dim).transpose(2, 0, 1, 3)
    kv_cols = dec_kv.reshape(share, 2, HIGH, groups, head_dim).transpose(3, 0, 2, 1, 4)
    cols = jnp.concatenate(
        [q_cols.reshape(groups, share, -1), kv_cols.reshape(groups, share, -1)], 2
    )
    cols = jnp.concatenate([cols] * HIGH, 0)
    w_heads = exchange(cols, "section").reshape(width, -1)
    wq = w_heads[:, : 2 * head_dim].T
    w_pairs = w_heads[:, 2 * head_dim :]
    far_rows = moved(dec_out, high=1)
    wo = jnp.where(
        high == 0,
        jnp.concatenate([dec_out, far_rows], 0),
        jnp.concatenate([far_rows, dec_out], 0),
    )
    own_pairs = jnp.dot(latent, w_pairs, preferred_element_type=f32).astype(bf16)
    pairs = gather_small(own_pairs, "ray").reshape(count * rows, -1)

    seen, pairs, wq, wo, ring[1], ring[-1], partner[0] = lax.optimization_barrier(
        (seen, pairs, wq, wo, ring[1], ring[-1], partner[0])
    )
    far = (moved(ring[1][0], along=1), moved(ring[-1][1], along=-1))
    partner[1], partner[-1] = moved(ring[1], core=1), moved(ring[-1], core=1)
    packed = jnp.dot(
        seen, enc_qkv[0].reshape(width, 3 * local_width), preferred_element_type=f32
    ).astype(bf16)
    mixed = attend_heads(packed, head_dim)
    attn = jnp.dot(mixed, enc_out[0], preferred_element_type=f32).astype(bf16)
    attn_rows = lax.psum_scatter(attn, "ray", scatter_dimension=0, tiled=True)

    pairs, partner[1], wo = lax.optimization_barrier((pairs, partner[1], wo, attn))[:3]
    wo_line = [wo, moved(wo, along=1), moved(wo, along=-1), moved(wo, along=2)]
    mixed_a, sums, proj = attend_rays(
        [ring[0], partner[0], ring[1], partner[1]], wq, wo, pairs, (), f32
    )
    sums, partner[-1], far, wo_line = lax.optimization_barrier((sums, partner[-1], far, wo_line))
    ring[2] = jnp.stack(far)
    partner[2] = moved(ring[2], core=1)
    wo_line = jnp.concatenate(wo_line, 0)
    wo_other = moved(wo_line, core=1)
    mixed_b, sums, proj = attend_rays(
        [ring[-1], partner[-1], ring[2], partner[2]], wq, wo, pairs, (sums, proj), bf16
    )
    attn_rows, wo_other = lax.optimization_barrier((attn_rows, wo_other, proj, sums))[:2]
    hidden = (tokens.astype(f32) + attn_rows.astype(f32)).astype(bf16)
    normed_two = layer_norm(hidden, enc_ln2[0]).astype(bf16)
    seen_two = lax.all_gather(normed_two, "ray", axis=0, tiled=True)
    mixed_a, mixed_b, sums, proj = lax.optimization_barrier(
        (mixed_a, mixed_b, sums, proj, normed_two)
    )[:4]

    proj = proj.reshape(count, 2 * head_dim // count, 4, width // 4).transpose(0, 2, 1, 3)
    proj = proj.reshape(count, -1, width // 4)
    both = exchange(jnp.concatenate([sums.reshape(count, rows, -1), proj], 1), "ray")
    both = jnp.sum(both.astype(f32), 0)
    pair_sum, term = both[:rows].astype(bf16), both[rows:]
    term = term + moved(term, high=1)
    term = term + lax.ppermute(term, "dp", [(0, 1), (1, 0)])
    term = gather_small(term.astype(bf16), "ray").reshape(count, 4, -1, width // 4)
    term = term.transpose(0, 2, 1, 3).reshape(2 * head_dim, width)

    blocks = [mixed_a[0], mixed_a[1], mixed_a[2], mixed_a[3]]
    blocks += [mixed_b[0], mixed_b[1], mixed_b[2], mixed_b[3]]
    back = {(k, c): blocks[2 * i + c] for i, k in enumerate(steps) for c in range(CORES)}
    mixed_t = {}
    for k in steps:
        for c in range(CORES):
            source = back[-k if k != 2 else 2, c]
            mixed_t[k, c] = moved(source, along=k, core=c) if k or c else source
    latent_part = lax.dot_general(pair_sum, w_pairs, NT, preferred_element_type=f32).astype(bf16)

    seen_two, term, latent_part = lax.optimization_barrier(
        (seen_two, term, latent_part, *mixed_t.values())
    )[:3]
    upper = jax.nn.gelu(
        jnp.dot(seen_two, enc_up[0], preferred_element_type=f32), approximate=True
    ).astype(bf16)
    lower = jnp.dot(upper, enc_down[0], preferred_element_type=f32).astype(bf16)
    lower_rows = lax.psum_scatter(lower, "ray", scatter_dimension=0, tiled=True)

    half = term.shape[0] // 2
    grads = {0: term, 1: moved(term, along=1), -1: moved(term, along=-1)}
    term, latent_part = lax.optimization_barrier((term, latent_part, lower))[:2]
    grads[2] = jnp.concatenate(
        [moved(grads[1][:half], along=1), moved(grads[-1][half:], along=-1)], 0
    )
    grads = jnp.stack([grads[k] for k in steps])
    where = [(place - k) % line * CORES + (core ^ c) for c in range(CORES) for k in steps]

    latent_part = exchange(latent_part.reshape(sections, -1, width), "section")
    latent_rows = jnp.sum(latent_part.astype(f32), 0).astype(bf16)
    latent_grad = gather_small(latent_rows, "section").reshape(rows, width)

    features = queries.astype(f32)
    for c, w_mix in ((0, wo_line), (1, wo_other)):
        side = jnp.concatenate([mixed_t[k, c] for k in steps], 0)
        features = features + lax.dot_general(side, w_mix, TN, preferred_element_type=f32)
    features = features.astype(bf16)
    other_grads = moved(grads, core=1)
    out_grad = placed([grads, other_grads], jnp.stack(where).astype(jnp.int32)).reshape(width, width)

    lower_rows = after(lower_rows, latent_rows, features, out_grad)
    layer_out = (hidden.astype(f32) + lower_rows.astype(f32)).astype(bf16)
    handed = lax.ppermute(layer_out, "section", [(i, i + 1) for i in range(sections - 1)])
    columns = width // sections
    finished = exchange(layer_out.T.reshape(sections, columns, rows), "section")[sections - 1].T
    return (handed[None, None], finished[None], features[None], latent_grad[None], out_grad)


def solution(mesh):
    return jax.shard_map(
        local,
        mesh=mesh,
        in_specs=(
            P("section", "dp", "ray", None),
            P("section", None),
            P("section", None, None, "ray"),
            P("section", "ray", None),
            P("section", None),
            P("section", None, "ray"),
            P("section", "ray", None),
            P("dp", "ray", None),
            P("dp", ("section", "ray"), None),
            P("section", None),
            P("section", None, None),
            P("section", None),
            P("dp", ("section", "ray"), None),
        ),
        out_specs=(
            P("section", "dp", "ray", None),
            P("dp", "ray", "section"),
            P("dp", ("section", "ray"), None),
            P("dp", "ray", None),
            P(),
        ),
        check_vma=False,
    )
```

```python
import functools
import math

import jax
import jax.numpy as jnp
from jax import lax
from jax.experimental import pallas as pl
from jax.experimental.pallas import tpu as pltpu
from jax.sharding import PartitionSpec as P

HEADS = 16


def layer_norm(values, gain):
    values = values.astype(jnp.float32)
    center = values - jnp.mean(values, -1, keepdims=True)
    spread = jnp.mean(center * center, -1, keepdims=True)
    return center * lax.rsqrt(spread + 1e-05) * gain


def softmax_rows(scores):
    top = jnp.max(scores, -1, keepdims=True)
    expo = jnp.exp(scores - top)
    return expo / jnp.sum(expo, -1, keepdims=True)


def attend_heads(packed, head_dim):
    length = packed.shape[0]
    heads = packed.shape[1] // (3 * head_dim)
    split = packed.reshape(length, 3, heads, head_dim)
    scores = jnp.einsum(
        "qhd,khd->hqk", split[:, 0], split[:, 1], preferred_element_type=jnp.float32
    ) / math.sqrt(head_dim)
    probs = softmax_rows(scores).astype(jnp.bfloat16)
    mixed = jnp.einsum("hqk,khd->qhd", probs, split[:, 2], preferred_element_type=jnp.float32)
    return mixed.astype(jnp.bfloat16).reshape(length, heads * head_dim)


NT = (((1,), (1,)), ((), ()))
TN = (((0,), (0,)), ((), ()))
CORES = 2
HIGH = 2


def moved(value, high=0, along=0, core=0):
    count = lax.axis_size("section")
    line = count // (CORES * HIGH)
    pairs = []
    for source in range(count):
        c, x, y = source % CORES, source // CORES % line, source // (CORES * line)
        target = ((y ^ high) * line + (x + along) % line) * CORES + (c ^ core)
        pairs.append((source, target))
    return lax.ppermute(value, "section", pairs)


def exchange(blocks, axis):
    return lax.all_to_all(blocks, axis, split_axis=0, concat_axis=0, tiled=True)


def gather_small(value, axis):
    count = lax.axis_size(axis)
    return exchange(jnp.broadcast_to(value[None], (count,) + value.shape), axis)


def after(value, *others):
    return lax.optimization_barrier((value,) + others)[0]


def rays_kernel(blocks, carried, *refs):
    ray_refs, (wq_ref, wo_ref, pairs_ref), refs = refs[:blocks], refs[blocks : blocks + 3], refs[blocks + 3 :]
    if carried:
        (sums_in, proj_in), refs = refs[:2], refs[2:]
    mixed_ref, sums_ref, proj_ref, rays, query, grad, pairs_t, sums, proj = refs
    block, head = pl.program_id(0), pl.program_id(1)
    dim = wq_ref.shape[0] // 2
    scale = 1.0 / math.sqrt(dim)

    @pl.when((block == 0) & (head == 0))
    def _():
        if carried:
            sums[...] = sums_in[...]
            proj[...] = proj_in[...]
        else:
            sums[...] = jnp.zeros_like(sums)
            proj[...] = jnp.zeros_like(proj)
        for i in range(2):
            pairs_t[i] = pairs_ref[:, 2 * dim * i : 2 * dim * (i + 1)].T

    for i in range(blocks):

        @pl.when((block == i) & (head == 0))
        def _(i=i):
            rays[...] = ray_refs[i][...]

    @pl.when(head == 0)
    def _():
        both_query = lax.dot_general(wq_ref[...], rays[0], NT, preferred_element_type=jnp.float32)
        both_grad = lax.dot_general(wo_ref[...], rays[1], NT, preferred_element_type=jnp.float32)
        both_query, both_grad = both_query.astype(jnp.bfloat16), both_grad.astype(jnp.bfloat16)
        zero = jnp.zeros((dim, both_query.shape[1]), jnp.bfloat16)
        for i in range(2):
            query[i, :dim] = both_query[dim * i : dim * (i + 1)]
            query[i, dim:] = zero
            grad[i, :dim] = zero
            grad[i, dim:] = both_grad[dim * i : dim * (i + 1)]

    lanes = pl.ds(pl.multiple_of(2 * dim * head, 2 * dim), 2 * dim)
    pairs = pairs_ref[:, lanes]
    scores = jnp.dot(pairs, query[head], preferred_element_type=jnp.float32)
    top = jnp.max(scores, 0, keepdims=True)
    expo = jnp.exp((scores - top) * scale)
    probs = expo * (1.0 / jnp.sum(expo, 0, keepdims=True))
    low = probs.astype(jnp.bfloat16)
    mixed = jnp.dot(pairs_t[head, dim:], low, preferred_element_type=jnp.float32)
    mixed_ref[block, pl.ds(pl.multiple_of(dim * head, dim), dim), :] = mixed.astype(jnp.bfloat16)
    prob_grad = jnp.dot(pairs, grad[head], preferred_element_type=jnp.float32)
    delta = jnp.sum(probs * prob_grad, 0, keepdims=True)
    score_grad = (probs * (prob_grad - delta) * scale).astype(jnp.bfloat16)
    part = lax.dot_general(score_grad, query[head], NT, preferred_element_type=jnp.float32)
    part = part + lax.dot_general(low, grad[head], NT, preferred_element_type=jnp.float32)
    sums[:, lanes] += part.astype(jnp.bfloat16).astype(jnp.float32)

    @pl.when(head == 1)
    def _():
        proj[...] += jnp.dot(mixed_ref[block], rays[1], preferred_element_type=jnp.float32)

    @pl.when((head == 1) & (block == blocks - 1))
    def _():
        sums_ref[...] = sums[...].astype(sums_ref.dtype)
        proj_ref[...] = proj[...].astype(proj_ref.dtype)


def attend_rays(rays, wq, wo, pairs, carry, kind):
    _, width, model = rays[0].shape
    length, columns = pairs.shape
    both, blocks = wq.shape[0], len(rays)
    work = 2 * blocks * width * length
    operands = [*rays, wq, wo, pairs, *carry]

    def whole(shape):
        return pl.BlockSpec(shape, lambda i, j: (0,) * len(shape))

    shapes = [(blocks, both, width), (length, columns), (both, model)]
    kinds = [jnp.bfloat16, kind, kind]
    return pl.pallas_call(
        functools.partial(rays_kernel, blocks, bool(carry)),
        grid=(blocks, 2),
        in_specs=[whole(x.shape) for x in operands],
        out_specs=[whole(x) for x in shapes],
        out_shape=[jax.ShapeDtypeStruct(x, k) for x, k in zip(shapes, kinds)],
        scratch_shapes=[
            pltpu.VMEM(rays[0].shape, jnp.bfloat16),
            pltpu.VMEM((2, both, width), jnp.bfloat16),
            pltpu.VMEM((2, both, width), jnp.bfloat16),
            pltpu.VMEM((2, both, length), jnp.bfloat16),
            pltpu.VMEM((length, columns), jnp.float32),
            pltpu.VMEM((both, model), jnp.float32),
        ],
        compiler_params=pltpu.CompilerParams(dimension_semantics=("arbitrary", "arbitrary")),
        cost_estimate=pl.CostEstimate(
            flops=8 * both * work, transcendentals=work, bytes_accessed=4 * blocks * width * model
        ),
    )(*operands)


def place_kernel(where_ref, *refs):
    out_ref = refs[-1]
    for i, ref in enumerate(refs[:-1]):
        steps, rows = ref.shape[0], ref.shape[1] // 2
        for k in range(steps):
            for j in range(2):
                out_ref[j, where_ref[steps * i + k]] = ref[k, rows * j : rows * (j + 1)].astype(jnp.float32)


def placed(parts, where):
    steps, rows, model = parts[0].shape
    out = (2, steps * len(parts), rows // 2, model)
    return pl.pallas_call(
        place_kernel,
        grid_spec=pltpu.PrefetchScalarGridSpec(
            num_scalar_prefetch=1,
            grid=(1,),
            in_specs=[pl.BlockSpec((steps, rows, model), lambda i, w: (0, 0, 0)) for _ in parts],
            out_specs=pl.BlockSpec(out, lambda i, w: (0, 0, 0, 0)),
        ),
        out_shape=jax.ShapeDtypeStruct(out, jnp.float32),
    )(where, *parts)


def local(
    section_tokens,
    enc_ln1,
    enc_qkv,
    enc_out,
    enc_ln2,
    enc_up,
    enc_down,
    set_latent,
    ray_queries,
    dec_query,
    dec_kv,
    dec_out,
    feature_grad,
):
    tokens = section_tokens[0, 0]
    width = tokens.shape[1]
    head_dim = width // HEADS
    local_width = enc_out.shape[1]
    sections = lax.axis_size("section")
    count = lax.axis_size("ray")
    groups = sections // HIGH
    line = groups // CORES
    latent = set_latent[0]
    queries = ray_queries[0]
    cotangent = feature_grad[0]
    rows, share = tokens.shape[0], dec_query.shape[0]
    f32, bf16 = jnp.float32, jnp.bfloat16
    here = lax.axis_index("section")
    core, place, high = here % CORES, here // CORES % line, here // groups

    normed = layer_norm(tokens, enc_ln1[0]).astype(bf16)
    seen = lax.all_gather(normed, "ray", axis=0, tiled=True)

    steps = (0, 1, -1, 2)
    own = jnp.stack([queries, cotangent])
    own = after(own, normed)
    ring = {0: own, 1: moved(own, along=1), -1: moved(own, along=-1)}
    partner = {0: moved(own, core=1)}

    q_cols = dec_query.reshape(share, HIGH, groups, head_dim).transpose(2, 0, 1, 3)
    kv_cols = dec_kv.reshape(share, 2, HIGH, groups, head_dim).transpose(3, 0, 2, 1, 4)
    cols = jnp.concatenate(
        [q_cols.reshape(groups, share, -1), kv_cols.reshape(groups, share, -1)], 2
    )
    cols = jnp.concatenate([cols] * HIGH, 0)
    w_heads = exchange(cols, "section").reshape(width, -1)
    wq = w_heads[:, : 2 * head_dim].T
    w_pairs = w_heads[:, 2 * head_dim :]
    far_rows = moved(dec_out, high=1)
    wo = jnp.where(
        high == 0,
        jnp.concatenate([dec_out, far_rows], 0),
        jnp.concatenate([far_rows, dec_out], 0),
    )
    own_pairs = jnp.dot(latent, w_pairs, preferred_element_type=f32).astype(bf16)
    pairs = gather_small(own_pairs, "ray").reshape(count * rows, -1)

    seen, ring[1], ring[-1], partner[0] = lax.optimization_barrier(
        (seen, ring[1], ring[-1], partner[0], own_pairs)
    )[:4]
    far = (moved(ring[1][0], along=1), moved(ring[-1][1], along=-1))
    partner[1], partner[-1] = moved(ring[1], core=1), moved(ring[-1], core=1)
    packed = jnp.dot(
        seen, enc_qkv[0].reshape(width, 3 * local_width), preferred_element_type=f32
    ).astype(bf16)
    packed, pairs, wo, wq = lax.optimization_barrier((packed, pairs, wo, wq))
    mixed = attend_heads(packed, head_dim)
    attn = jnp.dot(mixed, enc_out[0], preferred_element_type=f32).astype(bf16)
    attn_rows = lax.psum_scatter(attn, "ray", scatter_dimension=0, tiled=True)

    pairs, partner[1], wo = lax.optimization_barrier((pairs, partner[1], wo, attn))[:3]
    wo_line = [wo, moved(wo, along=1), moved(wo, along=-1), moved(wo, along=2)]
    mixed_a, sums, proj = attend_rays(
        [ring[0], partner[0], ring[1], partner[1]], wq, wo, pairs, (), f32
    )
    sums, partner[-1], far = lax.optimization_barrier((sums, partner[-1], far))
    ring[2] = jnp.stack(far)
    partner[2] = moved(ring[2], core=1)
    mixed_b, sums, proj = attend_rays(
        [ring[-1], partner[-1]], wq, wo, pairs, (sums, proj), f32
    )
    attn_rows, partner[2], wo_line = lax.optimization_barrier(
        (attn_rows, partner[2], wo_line, proj, sums)
    )[:3]
    hidden = (tokens.astype(f32) + attn_rows.astype(f32)).astype(bf16)
    normed_two = layer_norm(hidden, enc_ln2[0]).astype(bf16)
    seen_two = lax.all_gather(normed_two, "ray", axis=0, tiled=True)
    proj, wo_line = lax.optimization_barrier((proj, wo_line, normed_two))[:2]
    wo_line = jnp.concatenate(wo_line, 0)
    wo_other = moved(wo_line, core=1)
    mixed_c, sums, proj = attend_rays(
        [ring[2], partner[2]], wq, wo, pairs, (sums, proj), bf16
    )

    proj = proj.reshape(count, -1, width)
    term = jnp.sum(exchange(proj, "ray").astype(f32), 0)
    term = term + moved(term, high=1)
    term = term + lax.ppermute(term, "dp", [(0, 1), (1, 0)])
    term = gather_small(term.astype(bf16), "ray").reshape(2 * head_dim, width)

    blocks = [mixed_a[0], mixed_a[1], mixed_a[2], mixed_a[3], mixed_b[0], mixed_b[1]]
    blocks += [mixed_c[0], mixed_c[1]]
    back = {(k, c): blocks[2 * i + c] for i, k in enumerate(steps) for c in range(CORES)}
    mixed_t = {}
    for k in steps:
        for c in range(CORES):
            source = back[-k if k != 2 else 2, c]
            mixed_t[k, c] = moved(source, along=k, core=c) if k or c else source
    features = queries.astype(f32)
    for c, w_mix in ((0, wo_line), (1, wo_other)):
        side = jnp.concatenate([mixed_t[k, c] for k in steps], 0)
        features = features + lax.dot_general(side, w_mix, TN, preferred_element_type=f32)
    features = features.astype(bf16)

    seen_two, term = lax.optimization_barrier((seen_two, term, features))[:2]
    upper = jax.nn.gelu(
        jnp.dot(seen_two, enc_up[0], preferred_element_type=f32), approximate=True
    ).astype(bf16)
    lower = jnp.dot(upper, enc_down[0], preferred_element_type=f32).astype(bf16)
    lower_rows = lax.psum_scatter(lower, "ray", scatter_dimension=0, tiled=True)

    half = term.shape[0] // 2
    grads = {0: term, 1: moved(term, along=1), -1: moved(term, along=-1)}
    grads[2] = jnp.concatenate(
        [moved(grads[1][:half], along=1), moved(grads[-1][half:], along=-1)], 0
    )
    grads = jnp.stack([grads[k] for k in steps])
    where = [(place - k) % line * CORES + (core ^ c) for c in range(CORES) for k in steps]

    pair_sum = exchange(after(sums, lower).reshape(count, rows, -1), "ray")
    pair_sum = jnp.sum(pair_sum.astype(f32), 0).astype(bf16)
    latent_part = lax.dot_general(pair_sum, w_pairs, NT, preferred_element_type=f32).astype(bf16)
    latent_part = exchange(latent_part.reshape(sections, -1, width), "section")
    latent_rows = jnp.sum(latent_part.astype(f32), 0).astype(bf16)
    latent_grad = gather_small(latent_rows, "section").reshape(rows, width)
    other_grads = moved(grads, core=1)
    out_grad = placed([grads, other_grads], jnp.stack(where).astype(jnp.int32)).reshape(width, width)

    lower_rows = after(lower_rows, latent_rows, out_grad)
    layer_out = (hidden.astype(f32) + lower_rows.astype(f32)).astype(bf16)
    handed = lax.ppermute(layer_out, "section", [(i, i + 1) for i in range(sections - 1)])
    columns = width // sections
    finished = exchange(layer_out.T.reshape(sections, columns, rows), "section")[sections - 1].T
    return (handed[None, None], finished[None], features[None], latent_grad[None], out_grad)


def solution(mesh):
    return jax.shard_map(
        local,
        mesh=mesh,
        in_specs=(
            P("section", "dp", "ray", None),
            P("section", None),
            P("section", None, None, "ray"),
            P("section", "ray", None),
            P("section", None),
            P("section", None, "ray"),
            P("section", "ray", None),
            P("dp", "ray", None),
            P("dp", ("section", "ray"), None),
            P("section", None),
            P("section", None, None),
            P("section", None),
            P("dp", ("section", "ray"), None),
        ),
        out_specs=(
            P("section", "dp", "ray", None),
            P("dp", "ray", "section"),
            P("dp", ("section", "ray"), None),
            P("dp", "ray", None),
            P(),
        ),
        check_vma=False,
    )
```

```python
import functools
import math

import jax
import jax.numpy as jnp
from jax import lax
from jax.experimental import pallas as pl
from jax.experimental.pallas import tpu as pltpu
from jax.sharding import PartitionSpec as P

HEADS = 16


def layer_norm(values, gain):
    values = values.astype(jnp.float32)
    center = values - jnp.mean(values, -1, keepdims=True)
    spread = jnp.mean(center * center, -1, keepdims=True)
    return center * lax.rsqrt(spread + 1e-05) * gain


def softmax_rows(scores):
    top = jnp.max(scores, -1, keepdims=True)
    expo = jnp.exp(scores - top)
    return expo / jnp.sum(expo, -1, keepdims=True)


def attend_heads(packed, head_dim):
    length = packed.shape[0]
    heads = packed.shape[1] // (3 * head_dim)
    split = packed.reshape(length, 3, heads, head_dim)
    scores = jnp.einsum(
        "qhd,khd->hqk", split[:, 0], split[:, 1], preferred_element_type=jnp.float32
    ) / math.sqrt(head_dim)
    probs = softmax_rows(scores).astype(jnp.bfloat16)
    mixed = jnp.einsum("hqk,khd->qhd", probs, split[:, 2], preferred_element_type=jnp.float32)
    return mixed.astype(jnp.bfloat16).reshape(length, heads * head_dim)


NT = (((1,), (1,)), ((), ()))
TN = (((0,), (0,)), ((), ()))
CORES = 2
HIGH = 2


def moved(value, high=0, along=0, core=0):
    count = lax.axis_size("section")
    line = count // (CORES * HIGH)
    pairs = []
    for source in range(count):
        c, x, y = source % CORES, source // CORES % line, source // (CORES * line)
        target = ((y ^ high) * line + (x + along) % line) * CORES + (c ^ core)
        pairs.append((source, target))
    return lax.ppermute(value, "section", pairs)


def exchange(blocks, axis):
    return lax.all_to_all(blocks, axis, split_axis=0, concat_axis=0, tiled=True)


def gather_small(value, axis):
    count = lax.axis_size(axis)
    return exchange(jnp.broadcast_to(value[None], (count,) + value.shape), axis)


def after(value, *others):
    return lax.optimization_barrier((value,) + others)[0]


def rays_kernel(blocks, carried, *refs):
    ray_refs, (wq_ref, wo_ref, pairs_ref), refs = refs[:blocks], refs[blocks : blocks + 3], refs[blocks + 3 :]
    if carried:
        (sums_in, proj_in), refs = refs[:2], refs[2:]
    mixed_ref, sums_ref, proj_ref, rays, query, grad, pairs_t, sums, proj = refs
    block, head = pl.program_id(0), pl.program_id(1)
    dim = wq_ref.shape[0] // 2
    scale = 1.0 / math.sqrt(dim)

    @pl.when((block == 0) & (head == 0))
    def _():
        if carried:
            sums[...] = sums_in[...]
            proj[...] = proj_in[...]
        else:
            sums[...] = jnp.zeros_like(sums)
            proj[...] = jnp.zeros_like(proj)
        for i in range(2):
            pairs_t[i] = pairs_ref[:, 2 * dim * i : 2 * dim * (i + 1)].T

    for i in range(blocks):

        @pl.when((block == i) & (head == 0))
        def _(i=i):
            rays[...] = ray_refs[i][...]

    @pl.when(head == 0)
    def _():
        both_query = lax.dot_general(wq_ref[...], rays[0], NT, preferred_element_type=jnp.float32)
        both_grad = lax.dot_general(wo_ref[...], rays[1], NT, preferred_element_type=jnp.float32)
        both_query, both_grad = both_query.astype(jnp.bfloat16), both_grad.astype(jnp.bfloat16)
        zero = jnp.zeros((dim, both_query.shape[1]), jnp.bfloat16)
        for i in range(2):
            query[i, :dim] = both_query[dim * i : dim * (i + 1)]
            query[i, dim:] = zero
            grad[i, :dim] = zero
            grad[i, dim:] = both_grad[dim * i : dim * (i + 1)]

    lanes = pl.ds(pl.multiple_of(2 * dim * head, 2 * dim), 2 * dim)
    pairs = pairs_ref[:, lanes]
    scores = jnp.dot(pairs, query[head], preferred_element_type=jnp.float32)
    top = jnp.max(scores, 0, keepdims=True)
    expo = jnp.exp((scores - top) * scale)
    probs = expo * (1.0 / jnp.sum(expo, 0, keepdims=True))
    low = probs.astype(jnp.bfloat16)
    mixed = jnp.dot(pairs_t[head, dim:], low, preferred_element_type=jnp.float32)
    mixed_ref[block, pl.ds(pl.multiple_of(dim * head, dim), dim), :] = mixed.astype(jnp.bfloat16)
    prob_grad = jnp.dot(pairs, grad[head], preferred_element_type=jnp.float32)
    delta = jnp.sum(probs * prob_grad, 0, keepdims=True)
    score_grad = (probs * (prob_grad - delta) * scale).astype(jnp.bfloat16)
    part = lax.dot_general(score_grad, query[head], NT, preferred_element_type=jnp.float32)
    part = part + lax.dot_general(low, grad[head], NT, preferred_element_type=jnp.float32)
    sums[:, lanes] += part.astype(jnp.bfloat16).astype(jnp.float32)

    @pl.when(head == 1)
    def _():
        proj[...] += jnp.dot(mixed_ref[block], rays[1], preferred_element_type=jnp.float32)

    @pl.when((head == 1) & (block == blocks - 1))
    def _():
        sums_ref[...] = sums[...].astype(sums_ref.dtype)
        proj_ref[...] = proj[...].astype(proj_ref.dtype)


def attend_rays(rays, wq, wo, pairs, carry, kind):
    _, width, model = rays[0].shape
    length, columns = pairs.shape
    both, blocks = wq.shape[0], len(rays)
    work = 2 * blocks * width * length
    operands = [*rays, wq, wo, pairs, *carry]

    def whole(shape):
        return pl.BlockSpec(shape, lambda i, j: (0,) * len(shape))

    shapes = [(blocks, both, width), (length, columns), (both, model)]
    kinds = [jnp.bfloat16, kind, kind]
    return pl.pallas_call(
        functools.partial(rays_kernel, blocks, bool(carry)),
        grid=(blocks, 2),
        in_specs=[whole(x.shape) for x in operands],
        out_specs=[whole(x) for x in shapes],
        out_shape=[jax.ShapeDtypeStruct(x, k) for x, k in zip(shapes, kinds)],
        scratch_shapes=[
            pltpu.VMEM(rays[0].shape, jnp.bfloat16),
            pltpu.VMEM((2, both, width), jnp.bfloat16),
            pltpu.VMEM((2, both, width), jnp.bfloat16),
            pltpu.VMEM((2, both, length), jnp.bfloat16),
            pltpu.VMEM((length, columns), jnp.float32),
            pltpu.VMEM((both, model), jnp.float32),
        ],
        compiler_params=pltpu.CompilerParams(dimension_semantics=("arbitrary", "arbitrary")),
        cost_estimate=pl.CostEstimate(
            flops=8 * both * work, transcendentals=work, bytes_accessed=4 * blocks * width * model
        ),
    )(*operands)


def place_kernel(where_ref, *refs):
    out_ref = refs[-1]
    for i, ref in enumerate(refs[:-1]):
        steps, rows = ref.shape[0], ref.shape[1] // 2
        for k in range(steps):
            for j in range(2):
                out_ref[j, where_ref[steps * i + k]] = ref[k, rows * j : rows * (j + 1)].astype(jnp.float32)


def placed(parts, where):
    steps, rows, model = parts[0].shape
    out = (2, steps * len(parts), rows // 2, model)
    return pl.pallas_call(
        place_kernel,
        grid_spec=pltpu.PrefetchScalarGridSpec(
            num_scalar_prefetch=1,
            grid=(1,),
            in_specs=[pl.BlockSpec((steps, rows, model), lambda i, w: (0, 0, 0)) for _ in parts],
            out_specs=pl.BlockSpec(out, lambda i, w: (0, 0, 0, 0)),
        ),
        out_shape=jax.ShapeDtypeStruct(out, jnp.float32),
    )(where, *parts)


def local(
    section_tokens,
    enc_ln1,
    enc_qkv,
    enc_out,
    enc_ln2,
    enc_up,
    enc_down,
    set_latent,
    ray_queries,
    dec_query,
    dec_kv,
    dec_out,
    feature_grad,
):
    tokens = section_tokens[0, 0]
    width = tokens.shape[1]
    head_dim = width // HEADS
    local_width = enc_out.shape[1]
    sections = lax.axis_size("section")
    count = lax.axis_size("ray")
    groups = sections // HIGH
    line = groups // CORES
    latent = set_latent[0]
    queries = ray_queries[0]
    cotangent = feature_grad[0]
    rows, share = tokens.shape[0], dec_query.shape[0]
    f32, bf16 = jnp.float32, jnp.bfloat16
    here = lax.axis_index("section")
    core, place, high = here % CORES, here // CORES % line, here // groups

    normed = layer_norm(tokens, enc_ln1[0]).astype(bf16)
    seen = lax.all_gather(normed, "ray", axis=0, tiled=True)
    w_out = lax.all_gather(after(enc_out[0], normed), "ray", axis=0, tiled=True)

    steps = (0, 1, -1, 2)
    own = jnp.stack([queries, cotangent])
    own = after(own, normed)
    ring = {0: own, 1: moved(own, along=1), -1: moved(own, along=-1)}
    partner = {0: moved(own, core=1)}

    q_cols = dec_query.reshape(share, HIGH, groups, head_dim).transpose(2, 0, 1, 3)
    kv_cols = dec_kv.reshape(share, 2, HIGH, groups, head_dim).transpose(3, 0, 2, 1, 4)
    cols = jnp.concatenate(
        [q_cols.reshape(groups, share, -1), kv_cols.reshape(groups, share, -1)], 2
    )
    cols = jnp.concatenate([cols] * HIGH, 0)
    w_heads = exchange(cols, "section").reshape(width, -1)
    wq = w_heads[:, : 2 * head_dim].T
    w_pairs = w_heads[:, 2 * head_dim :]
    far_rows = moved(dec_out, high=1)
    wo = jnp.where(
        high == 0,
        jnp.concatenate([dec_out, far_rows], 0),
        jnp.concatenate([far_rows, dec_out], 0),
    )
    own_pairs = jnp.dot(latent, w_pairs, preferred_element_type=f32).astype(bf16)
    pairs = gather_small(own_pairs, "ray").reshape(count * rows, -1)

    seen, ring[1], ring[-1], partner[0] = lax.optimization_barrier(
        (seen, ring[1], ring[-1], partner[0], own_pairs)
    )[:4]
    far = (moved(ring[1][0], along=1), moved(ring[-1][1], along=-1))
    partner[1], partner[-1] = moved(ring[1], core=1), moved(ring[-1], core=1)
    packed = jnp.dot(
        seen, enc_qkv[0].reshape(width, 3 * local_width), preferred_element_type=f32
    ).astype(bf16)
    packed, pairs, wo, wq = lax.optimization_barrier((packed, pairs, wo, wq))
    mixed = attend_heads(packed, head_dim)
    mixed = mixed.reshape(count, rows, -1)
    columns = exchange(mixed, "ray")

    pairs, partner[1], wo = lax.optimization_barrier((pairs, partner[1], wo, mixed))[:3]
    mixed_a, sums, proj = attend_rays(
        [ring[0], partner[0], ring[1], partner[1]], wq, wo, pairs, (), f32
    )
    columns, w_out, sums, far = lax.optimization_barrier((columns, w_out, sums, far))
    attn = jnp.einsum(
        "rtc,rcd->rtd", columns, w_out.reshape(count, -1, width), preferred_element_type=f32
    ).astype(bf16)
    attn_rows = jnp.sum(attn.astype(f32), 0)
    hidden = (tokens.astype(f32) + attn_rows).astype(bf16)
    normed_two = layer_norm(hidden, enc_ln2[0]).astype(bf16)
    seen_two = lax.all_gather(normed_two, "ray", axis=0, tiled=True)
    far, wo_near = lax.optimization_barrier((far, wo, normed_two))[:2]
    ring[2] = jnp.stack(far)
    partner[2] = moved(ring[2], core=1)
    wo_line = [
        wo_near, moved(wo_near, along=1), moved(wo_near, along=-1), moved(wo_near, along=2)
    ]
    mixed_b, sums, proj = attend_rays(
        [ring[-1], partner[-1], ring[2], partner[2]], wq, wo, pairs, (sums, proj), bf16
    )
    wo_line, proj = lax.optimization_barrier((wo_line, proj))
    wo_line = jnp.concatenate(wo_line, 0)
    wo_other = moved(wo_line, core=1)

    term = exchange(proj.reshape(count, -1, width), "ray")

    blocks = [mixed_a[0], mixed_a[1], mixed_a[2], mixed_a[3]]
    blocks += [mixed_b[0], mixed_b[1], mixed_b[2], mixed_b[3]]
    back = {(k, c): blocks[2 * i + c] for i, k in enumerate(steps) for c in range(CORES)}
    mixed_t = {}
    for k in steps:
        for c in range(CORES):
            source = back[-k if k != 2 else 2, c]
            mixed_t[k, c] = moved(source, along=k, core=c) if k or c else source
    seen_two, wo_line, term = lax.optimization_barrier(
        (seen_two, wo_line, term, *mixed_t.values())
    )[:3]
    upper = jax.nn.gelu(
        jnp.dot(seen_two, enc_up[0], preferred_element_type=f32), approximate=True
    ).astype(bf16)
    lower = jnp.dot(upper, enc_down[0], preferred_element_type=f32).astype(bf16)
    lower_rows = lax.psum_scatter(lower, "ray", scatter_dimension=0, tiled=True)

    term, sums, wo_line, wo_other = lax.optimization_barrier(
        (term, sums, wo_line, wo_other, lower)
    )[:4]
    term = jnp.sum(term.astype(f32), 0)
    term = term + moved(term, high=1)
    term = term + lax.ppermute(term, "dp", [(0, 1), (1, 0)])
    term, sums = lax.optimization_barrier((term.astype(bf16), sums))
    pair_sum = exchange(sums.reshape(count, rows, -1), "ray")
    term = gather_small(term, "ray").reshape(2 * head_dim, width)
    features = queries.astype(f32)
    for c, w_mix in ((0, wo_line), (1, wo_other)):
        side = jnp.concatenate([mixed_t[k, c] for k in steps], 0)
        features = features + lax.dot_general(side, w_mix, TN, preferred_element_type=f32)
    features = features.astype(bf16)

    half = term.shape[0] // 2
    grads = {0: term, 1: moved(term, along=1), -1: moved(term, along=-1)}
    grads[2] = jnp.concatenate(
        [moved(grads[1][:half], along=1), moved(grads[-1][half:], along=-1)], 0
    )
    grads = jnp.stack([grads[k] for k in steps])
    where = [(place - k) % line * CORES + (core ^ c) for c in range(CORES) for k in steps]

    pair_sum = jnp.sum(after(pair_sum, grads).astype(f32), 0).astype(bf16)
    latent_part = lax.dot_general(pair_sum, w_pairs, NT, preferred_element_type=f32).astype(bf16)
    latent_part = exchange(latent_part.reshape(sections, -1, width), "section")
    latent_rows = jnp.sum(latent_part.astype(f32), 0).astype(bf16)
    latent_grad = gather_small(latent_rows, "section").reshape(rows, width)
    other_grads = moved(grads, core=1)
    out_grad = placed([grads, other_grads], jnp.stack(where).astype(jnp.int32)).reshape(width, width)

    lower_rows = after(lower_rows, latent_rows, features, out_grad)
    layer_out = (hidden.astype(f32) + lower_rows.astype(f32)).astype(bf16)
    handed = lax.ppermute(layer_out, "section", [(i, i + 1) for i in range(sections - 1)])
    finished = exchange(layer_out.T.reshape(sections, -1, rows), "section")[sections - 1].T
    return (handed[None, None], finished[None], features[None], latent_grad[None], out_grad)


def solution(mesh):
    return jax.shard_map(
        local,
        mesh=mesh,
        in_specs=(
            P("section", "dp", "ray", None),
            P("section", None),
            P("section", None, None, "ray"),
            P("section", "ray", None),
            P("section", None),
            P("section", None, "ray"),
            P("section", "ray", None),
            P("dp", "ray", None),
            P("dp", ("section", "ray"), None),
            P("section", None),
            P("section", None, None),
            P("section", None),
            P("dp", ("section", "ray"), None),
        ),
        out_specs=(
            P("section", "dp", "ray", None),
            P("dp", "ray", "section"),
            P("dp", ("section", "ray"), None),
            P("dp", "ray", None),
            P(),
        ),
        check_vma=False,
    )
```

```python
import functools
import math

import jax
import jax.numpy as jnp
from jax import lax
from jax.experimental import pallas as pl
from jax.experimental.pallas import tpu as pltpu
from jax.sharding import PartitionSpec as P

HEADS = 16


def layer_norm(values, gain):
    values = values.astype(jnp.float32)
    center = values - jnp.mean(values, -1, keepdims=True)
    spread = jnp.mean(center * center, -1, keepdims=True)
    return center * lax.rsqrt(spread + 1e-05) * gain


def softmax_rows(scores):
    top = jnp.max(scores, -1, keepdims=True)
    expo = jnp.exp(scores - top)
    return expo / jnp.sum(expo, -1, keepdims=True)


def attend_heads(packed, head_dim):
    length = packed.shape[0]
    heads = packed.shape[1] // (3 * head_dim)
    split = packed.reshape(length, 3, heads, head_dim)
    scores = jnp.einsum(
        "qhd,khd->hqk", split[:, 0], split[:, 1], preferred_element_type=jnp.float32
    ) / math.sqrt(head_dim)
    probs = softmax_rows(scores).astype(jnp.bfloat16)
    mixed = jnp.einsum("hqk,khd->qhd", probs, split[:, 2], preferred_element_type=jnp.float32)
    return mixed.astype(jnp.bfloat16).reshape(length, heads * head_dim)


NT = (((1,), (1,)), ((), ()))
TN = (((0,), (0,)), ((), ()))
CORES = 2
HIGH = 2


def moved(value, high=0, along=0, core=0):
    count = lax.axis_size("section")
    line = count // (CORES * HIGH)
    pairs = []
    for source in range(count):
        c, x, y = source % CORES, source // CORES % line, source // (CORES * line)
        target = ((y ^ high) * line + (x + along) % line) * CORES + (c ^ core)
        pairs.append((source, target))
    return lax.ppermute(value, "section", pairs)


def exchange(blocks, axis):
    return lax.all_to_all(blocks, axis, split_axis=0, concat_axis=0, tiled=True)


def gather_small(value, axis):
    count = lax.axis_size(axis)
    return exchange(jnp.broadcast_to(value[None], (count,) + value.shape), axis)


def after(value, *others):
    return lax.optimization_barrier((value,) + others)[0]


def rays_kernel(blocks, carried, *refs):
    ray_refs, (wq_ref, wo_ref, pairs_ref), refs = refs[:blocks], refs[blocks : blocks + 3], refs[blocks + 3 :]
    if carried:
        (sums_in, proj_in), refs = refs[:2], refs[2:]
    mixed_ref, sums_ref, proj_ref, rays, query, grad, pairs_t, sums, proj = refs
    block, head = pl.program_id(0), pl.program_id(1)
    dim = wq_ref.shape[0] // 2
    scale = 1.0 / math.sqrt(dim)

    @pl.when((block == 0) & (head == 0))
    def _():
        if carried:
            sums[...] = sums_in[...]
            proj[...] = proj_in[...]
        else:
            sums[...] = jnp.zeros_like(sums)
            proj[...] = jnp.zeros_like(proj)
        for i in range(2):
            pairs_t[i] = pairs_ref[:, 2 * dim * i : 2 * dim * (i + 1)].T

    for i in range(blocks):

        @pl.when((block == i) & (head == 0))
        def _(i=i):
            rays[...] = ray_refs[i][...]

    @pl.when(head == 0)
    def _():
        both_query = lax.dot_general(wq_ref[...], rays[0], NT, preferred_element_type=jnp.float32)
        both_grad = lax.dot_general(wo_ref[...], rays[1], NT, preferred_element_type=jnp.float32)
        both_query, both_grad = both_query.astype(jnp.bfloat16), both_grad.astype(jnp.bfloat16)
        zero = jnp.zeros((dim, both_query.shape[1]), jnp.bfloat16)
        for i in range(2):
            query[i, :dim] = both_query[dim * i : dim * (i + 1)]
            query[i, dim:] = zero
            grad[i, :dim] = zero
            grad[i, dim:] = both_grad[dim * i : dim * (i + 1)]

    lanes = pl.ds(pl.multiple_of(2 * dim * head, 2 * dim), 2 * dim)
    pairs = pairs_ref[:, lanes]
    scores = jnp.dot(pairs, query[head], preferred_element_type=jnp.float32)
    top = jnp.max(scores, 0, keepdims=True)
    expo = jnp.exp((scores - top) * scale)
    probs = expo * (1.0 / jnp.sum(expo, 0, keepdims=True))
    low = probs.astype(jnp.bfloat16)
    mixed = jnp.dot(pairs_t[head, dim:], low, preferred_element_type=jnp.float32)
    mixed_ref[block, pl.ds(pl.multiple_of(dim * head, dim), dim), :] = mixed.astype(jnp.bfloat16)
    prob_grad = jnp.dot(pairs, grad[head], preferred_element_type=jnp.float32)
    delta = jnp.sum(probs * prob_grad, 0, keepdims=True)
    score_grad = (probs * (prob_grad - delta) * scale).astype(jnp.bfloat16)
    part = lax.dot_general(score_grad, query[head], NT, preferred_element_type=jnp.float32)
    part = part + lax.dot_general(low, grad[head], NT, preferred_element_type=jnp.float32)
    sums[:, lanes] += part.astype(jnp.bfloat16).astype(jnp.float32)

    @pl.when(head == 1)
    def _():
        proj[...] += jnp.dot(mixed_ref[block], rays[1], preferred_element_type=jnp.float32)

    @pl.when((head == 1) & (block == blocks - 1))
    def _():
        sums_ref[...] = sums[...].astype(sums_ref.dtype)
        proj_ref[...] = proj[...].astype(proj_ref.dtype)


def attend_rays(rays, wq, wo, pairs, carry, kind):
    _, width, model = rays[0].shape
    length, columns = pairs.shape
    both, blocks = wq.shape[0], len(rays)
    work = 2 * blocks * width * length
    operands = [*rays, wq, wo, pairs, *carry]

    def whole(shape):
        return pl.BlockSpec(shape, lambda i, j: (0,) * len(shape))

    shapes = [(blocks, both, width), (length, columns), (both, model)]
    kinds = [jnp.bfloat16, kind, kind]
    return pl.pallas_call(
        functools.partial(rays_kernel, blocks, bool(carry)),
        grid=(blocks, 2),
        in_specs=[whole(x.shape) for x in operands],
        out_specs=[whole(x) for x in shapes],
        out_shape=[jax.ShapeDtypeStruct(x, k) for x, k in zip(shapes, kinds)],
        scratch_shapes=[
            pltpu.VMEM(rays[0].shape, jnp.bfloat16),
            pltpu.VMEM((2, both, width), jnp.bfloat16),
            pltpu.VMEM((2, both, width), jnp.bfloat16),
            pltpu.VMEM((2, both, length), jnp.bfloat16),
            pltpu.VMEM((length, columns), jnp.float32),
            pltpu.VMEM((both, model), jnp.float32),
        ],
        compiler_params=pltpu.CompilerParams(dimension_semantics=("arbitrary", "arbitrary")),
        cost_estimate=pl.CostEstimate(
            flops=8 * both * work, transcendentals=work, bytes_accessed=4 * blocks * width * model
        ),
    )(*operands)


def place_kernel(where_ref, *refs):
    out_ref = refs[-1]
    for i, ref in enumerate(refs[:-1]):
        steps, rows = ref.shape[0], ref.shape[1] // 2
        for k in range(steps):
            for j in range(2):
                out_ref[j, where_ref[steps * i + k]] = ref[k, rows * j : rows * (j + 1)].astype(jnp.float32)


def placed(parts, where):
    steps, rows, model = parts[0].shape
    out = (2, steps * len(parts), rows // 2, model)
    return pl.pallas_call(
        place_kernel,
        grid_spec=pltpu.PrefetchScalarGridSpec(
            num_scalar_prefetch=1,
            grid=(1,),
            in_specs=[pl.BlockSpec((steps, rows, model), lambda i, w: (0, 0, 0)) for _ in parts],
            out_specs=pl.BlockSpec(out, lambda i, w: (0, 0, 0, 0)),
        ),
        out_shape=jax.ShapeDtypeStruct(out, jnp.float32),
    )(where, *parts)


def local(
    section_tokens,
    enc_ln1,
    enc_qkv,
    enc_out,
    enc_ln2,
    enc_up,
    enc_down,
    set_latent,
    ray_queries,
    dec_query,
    dec_kv,
    dec_out,
    feature_grad,
):
    tokens = section_tokens[0, 0]
    width = tokens.shape[1]
    head_dim = width // HEADS
    local_width = enc_out.shape[1]
    sections = lax.axis_size("section")
    count = lax.axis_size("ray")
    groups = sections // HIGH
    line = groups // CORES
    latent = set_latent[0]
    queries = ray_queries[0]
    cotangent = feature_grad[0]
    rows, share = tokens.shape[0], dec_query.shape[0]
    f32, bf16 = jnp.float32, jnp.bfloat16
    here = lax.axis_index("section")
    core, place, high = here % CORES, here // CORES % line, here // groups

    normed = layer_norm(tokens, enc_ln1[0]).astype(bf16)
    seen = lax.all_gather(normed, "ray", axis=0, tiled=True)
    w_out = lax.all_gather(after(enc_out[0], normed), "ray", axis=0, tiled=True)

    steps = (0, 1, -1, 2)
    own = jnp.stack([queries, cotangent])
    own = after(own, normed)
    ring = {0: own, 1: moved(own, along=1), -1: moved(own, along=-1)}
    partner = {0: moved(own, core=1)}

    far_rows = moved(dec_out, high=1)
    wo = jnp.where(
        high == 0,
        jnp.concatenate([dec_out, far_rows], 0),
        jnp.concatenate([far_rows, dec_out], 0),
    )
    wo_line = jnp.concatenate(
        [wo, moved(wo, along=1), moved(wo, along=-1), moved(wo, along=2)], 0
    )

    q_cols = dec_query.reshape(share, HIGH, groups, head_dim).transpose(2, 0, 1, 3)
    kv_cols = dec_kv.reshape(share, 2, HIGH, groups, head_dim).transpose(3, 0, 2, 1, 4)
    cols = jnp.concatenate(
        [q_cols.reshape(groups, share, -1), kv_cols.reshape(groups, share, -1)], 2
    )
    cols = jnp.concatenate([cols] * HIGH, 0)
    w_heads = exchange(cols, "section").reshape(width, -1)
    wq = w_heads[:, : 2 * head_dim].T
    w_pairs = w_heads[:, 2 * head_dim :]
    own_pairs = jnp.dot(latent, w_pairs, preferred_element_type=f32).astype(bf16)
    pairs = gather_small(own_pairs, "ray").reshape(count * rows, -1)

    seen, ring[1], ring[-1], partner[0], own = lax.optimization_barrier(
        (seen, ring[1], ring[-1], partner[0], own, own_pairs, wo_line)
    )[:5]
    ring[2] = moved(own, along=2)
    partner[1], partner[-1] = moved(ring[1], core=1), moved(ring[-1], core=1)
    packed = jnp.dot(
        seen, enc_qkv[0].reshape(width, 3 * local_width), preferred_element_type=f32
    ).astype(bf16)
    packed, pairs, wo, wq = lax.optimization_barrier((packed, pairs, wo, wq))
    mixed = attend_heads(packed, head_dim)
    mixed = mixed.reshape(count, rows, -1)
    columns = exchange(mixed, "ray")

    pairs, partner[1], wo = lax.optimization_barrier((pairs, partner[1], wo, mixed))[:3]
    mixed_a, sums, proj = attend_rays(
        [ring[0], partner[0], ring[1], partner[1]], wq, wo, pairs, (), f32
    )
    columns, w_out, sums, ring[2] = lax.optimization_barrier((columns, w_out, sums, ring[2]))
    attn = jnp.einsum(
        "rtc,rcd->rtd", columns, w_out.reshape(count, -1, width), preferred_element_type=f32
    ).astype(bf16)
    attn_rows = jnp.sum(attn.astype(f32), 0)
    hidden = (tokens.astype(f32) + attn_rows).astype(bf16)
    normed_two = layer_norm(hidden, enc_ln2[0]).astype(bf16)
    seen_two = lax.all_gather(normed_two, "ray", axis=0, tiled=True)
    ring[2], wo_line = lax.optimization_barrier((ring[2], wo_line, normed_two))[:2]
    partner[2] = moved(ring[2], core=1)
    wo_other = moved(wo_line, core=1)
    mixed_b, sums, proj = attend_rays(
        [ring[-1], partner[-1], ring[2], partner[2]], wq, wo, pairs, (sums, proj), bf16
    )

    term = exchange(proj.reshape(count, -1, width), "ray")

    seen_two, term = lax.optimization_barrier((seen_two, term))
    upper = jax.nn.gelu(
        jnp.dot(seen_two, enc_up[0], preferred_element_type=f32), approximate=True
    ).astype(bf16)
    lower = jnp.dot(upper, enc_down[0], preferred_element_type=f32).astype(bf16)
    lower_rows = lax.psum_scatter(lower, "ray", scatter_dimension=0, tiled=True)

    term, sums, wo_line, wo_other = lax.optimization_barrier(
        (term, sums, wo_line, wo_other, lower)
    )[:4]
    term = jnp.sum(term.astype(f32), 0)
    term = term + moved(term, high=1)
    term = term + lax.ppermute(term, "dp", [(0, 1), (1, 0)])
    term, sums = lax.optimization_barrier((term.astype(bf16), sums))
    pair_sum = exchange(sums.reshape(count, rows, -1), "ray")
    term = gather_small(term, "ray").reshape(2 * head_dim, width)
    blocks = [mixed_a[0], mixed_a[1], mixed_a[2], mixed_a[3]]
    mixed_b = after(mixed_b, lower)
    blocks += [mixed_b[0], mixed_b[1], mixed_b[2], mixed_b[3]]
    back = {(k, c): blocks[2 * i + c] for i, k in enumerate(steps) for c in range(CORES)}
    mixed_t = {}
    for k in steps:
        for c in range(CORES):
            source = back[-k if k != 2 else 2, c]
            mixed_t[k, c] = moved(source, along=k, core=c) if k or c else source
    features = queries.astype(f32)
    for c, w_mix in ((0, wo_line), (1, wo_other)):
        side = jnp.concatenate([mixed_t[k, c] for k in steps], 0)
        features = features + lax.dot_general(side, w_mix, TN, preferred_element_type=f32)
    features = features.astype(bf16)

    half = term.shape[0] // 2
    grads = {0: term, 1: moved(term, along=1), -1: moved(term, along=-1)}
    grads[2] = jnp.concatenate(
        [moved(grads[1][:half], along=1), moved(grads[-1][half:], along=-1)], 0
    )
    grads = jnp.stack([grads[k] for k in steps])
    where = [(place - k) % line * CORES + (core ^ c) for c in range(CORES) for k in steps]

    pair_sum = jnp.sum(after(pair_sum, grads).astype(f32), 0).astype(bf16)
    latent_part = lax.dot_general(pair_sum, w_pairs, NT, preferred_element_type=f32).astype(bf16)
    latent_rows = exchange(latent_part.reshape(sections, -1, width), "section")
    latent_rows = jnp.sum(latent_rows.astype(f32), 0).astype(bf16)
    latent_grad = gather_small(latent_rows, "section").reshape(rows, width)
    other_grads = moved(grads, core=1)
    out_grad = placed([grads, other_grads], jnp.stack(where).astype(jnp.int32)).reshape(width, width)

    lower_rows = after(lower_rows, latent_part, features, out_grad)
    layer_out = (hidden.astype(f32) + lower_rows.astype(f32)).astype(bf16)
    handed = lax.ppermute(layer_out, "section", [(i, i + 1) for i in range(sections - 1)])
    finished = exchange(layer_out.T.reshape(sections, -1, rows), "section")[sections - 1].T
    return (handed[None, None], finished[None], features[None], latent_grad[None], out_grad)


def solution(mesh):
    return jax.shard_map(
        local,
        mesh=mesh,
        in_specs=(
            P("section", "dp", "ray", None),
            P("section", None),
            P("section", None, None, "ray"),
            P("section", "ray", None),
            P("section", None),
            P("section", None, "ray"),
            P("section", "ray", None),
            P("dp", "ray", None),
            P("dp", ("section", "ray"), None),
            P("section", None),
            P("section", None, None),
            P("section", None),
            P("dp", ("section", "ray"), None),
        ),
        out_specs=(
            P("section", "dp", "ray", None),
            P("dp", "ray", "section"),
            P("dp", ("section", "ray"), None),
            P("dp", "ray", None),
            P(),
        ),
        check_vma=False,
    )
```

```python
import functools
import math

import jax
import jax.numpy as jnp
from jax import lax
from jax.experimental import pallas as pl
from jax.experimental.pallas import tpu as pltpu
from jax.sharding import PartitionSpec as P

HEADS = 16


def layer_norm(values, gain):
    values = values.astype(jnp.float32)
    center = values - jnp.mean(values, -1, keepdims=True)
    spread = jnp.mean(center * center, -1, keepdims=True)
    return center * lax.rsqrt(spread + 1e-05) * gain


def softmax_rows(scores):
    top = jnp.max(scores, -1, keepdims=True)
    expo = jnp.exp(scores - top)
    return expo / jnp.sum(expo, -1, keepdims=True)


def attend_heads(packed, head_dim):
    length = packed.shape[0]
    heads = packed.shape[1] // (3 * head_dim)
    split = packed.reshape(length, 3, heads, head_dim)
    scores = jnp.einsum(
        "qhd,khd->hqk", split[:, 0], split[:, 1], preferred_element_type=jnp.float32
    ) / math.sqrt(head_dim)
    probs = softmax_rows(scores).astype(jnp.bfloat16)
    mixed = jnp.einsum("hqk,khd->qhd", probs, split[:, 2], preferred_element_type=jnp.float32)
    return mixed.astype(jnp.bfloat16).reshape(length, heads * head_dim)


NT = (((1,), (1,)), ((), ()))
TN = (((0,), (0,)), ((), ()))
CORES = 2
HIGH = 2


def moved(value, high=0, along=0, core=0):
    count = lax.axis_size("section")
    line = count // (CORES * HIGH)
    pairs = []
    for source in range(count):
        c, x, y = source % CORES, source // CORES % line, source // (CORES * line)
        target = ((y ^ high) * line + (x + along) % line) * CORES + (c ^ core)
        pairs.append((source, target))
    return lax.ppermute(value, "section", pairs)


def exchange(blocks, axis):
    return lax.all_to_all(blocks, axis, split_axis=0, concat_axis=0, tiled=True)


def gather_small(value, axis):
    count = lax.axis_size(axis)
    return exchange(jnp.broadcast_to(value[None], (count,) + value.shape), axis)


def after(value, *others):
    return lax.optimization_barrier((value,) + others)[0]


def rays_kernel(blocks, carried, *refs):
    ray_refs, (wq_ref, wo_ref, pairs_ref), refs = refs[:blocks], refs[blocks : blocks + 3], refs[blocks + 3 :]
    if carried:
        (sums_in, proj_in), refs = refs[:2], refs[2:]
    mixed_ref, sums_ref, proj_ref, rays, query, grad, pairs_t, sums, proj = refs
    block, head = pl.program_id(0), pl.program_id(1)
    dim = wq_ref.shape[0] // 2
    scale = 1.0 / math.sqrt(dim)

    @pl.when((block == 0) & (head == 0))
    def _():
        if carried:
            sums[...] = sums_in[...]
            proj[...] = proj_in[...]
        else:
            sums[...] = jnp.zeros_like(sums)
            proj[...] = jnp.zeros_like(proj)
        for i in range(2):
            pairs_t[i] = pairs_ref[:, 2 * dim * i : 2 * dim * (i + 1)].T

    for i in range(blocks):

        @pl.when((block == i) & (head == 0))
        def _(i=i):
            rays[...] = ray_refs[i][...]

    @pl.when(head == 0)
    def _():
        both_query = lax.dot_general(wq_ref[...], rays[0], NT, preferred_element_type=jnp.float32)
        both_grad = lax.dot_general(wo_ref[...], rays[1], NT, preferred_element_type=jnp.float32)
        both_query, both_grad = both_query.astype(jnp.bfloat16), both_grad.astype(jnp.bfloat16)
        zero = jnp.zeros((dim, both_query.shape[1]), jnp.bfloat16)
        for i in range(2):
            query[i, :dim] = both_query[dim * i : dim * (i + 1)]
            query[i, dim:] = zero
            grad[i, :dim] = zero
            grad[i, dim:] = both_grad[dim * i : dim * (i + 1)]

    lanes = pl.ds(pl.multiple_of(2 * dim * head, 2 * dim), 2 * dim)
    pairs = pairs_ref[:, lanes]
    scores = jnp.dot(pairs, query[head], preferred_element_type=jnp.float32)
    top = jnp.max(scores, 0, keepdims=True)
    expo = jnp.exp((scores - top) * scale)
    probs = expo * (1.0 / jnp.sum(expo, 0, keepdims=True))
    low = probs.astype(jnp.bfloat16)
    mixed = jnp.dot(pairs_t[head, dim:], low, preferred_element_type=jnp.float32)
    mixed_ref[block, pl.ds(pl.multiple_of(dim * head, dim), dim), :] = mixed.astype(jnp.bfloat16)
    prob_grad = jnp.dot(pairs, grad[head], preferred_element_type=jnp.float32)
    delta = jnp.sum(probs * prob_grad, 0, keepdims=True)
    score_grad = (probs * (prob_grad - delta) * scale).astype(jnp.bfloat16)
    part = lax.dot_general(score_grad, query[head], NT, preferred_element_type=jnp.float32)
    part = part + lax.dot_general(low, grad[head], NT, preferred_element_type=jnp.float32)
    sums[:, lanes] += part.astype(jnp.bfloat16).astype(jnp.float32)

    @pl.when(head == 1)
    def _():
        proj[...] += jnp.dot(mixed_ref[block], rays[1], preferred_element_type=jnp.float32)

    @pl.when((head == 1) & (block == blocks - 1))
    def _():
        sums_ref[...] = sums[...].astype(sums_ref.dtype)
        proj_ref[...] = proj[...].astype(proj_ref.dtype)


def attend_rays(rays, wq, wo, pairs, carry, kind):
    _, width, model = rays[0].shape
    length, columns = pairs.shape
    both, blocks = wq.shape[0], len(rays)
    work = 2 * blocks * width * length
    operands = [*rays, wq, wo, pairs, *carry]

    def whole(shape):
        return pl.BlockSpec(shape, lambda i, j: (0,) * len(shape))

    shapes = [(blocks, both, width), (length, columns), (both, model)]
    kinds = [jnp.bfloat16, kind, kind]
    return pl.pallas_call(
        functools.partial(rays_kernel, blocks, bool(carry)),
        grid=(blocks, 2),
        in_specs=[whole(x.shape) for x in operands],
        out_specs=[whole(x) for x in shapes],
        out_shape=[jax.ShapeDtypeStruct(x, k) for x, k in zip(shapes, kinds)],
        scratch_shapes=[
            pltpu.VMEM(rays[0].shape, jnp.bfloat16),
            pltpu.VMEM((2, both, width), jnp.bfloat16),
            pltpu.VMEM((2, both, width), jnp.bfloat16),
            pltpu.VMEM((2, both, length), jnp.bfloat16),
            pltpu.VMEM((length, columns), jnp.float32),
            pltpu.VMEM((both, model), jnp.float32),
        ],
        compiler_params=pltpu.CompilerParams(dimension_semantics=("arbitrary", "arbitrary")),
        cost_estimate=pl.CostEstimate(
            flops=8 * both * work, transcendentals=work, bytes_accessed=4 * blocks * width * model
        ),
    )(*operands)


def place_kernel(where_ref, *refs):
    out_ref = refs[-1]
    for i, ref in enumerate(refs[:-1]):
        steps, rows = ref.shape[0], ref.shape[1] // 2
        for k in range(steps):
            for j in range(2):
                out_ref[j, where_ref[steps * i + k]] = ref[k, rows * j : rows * (j + 1)].astype(jnp.float32)


def placed(parts, where):
    steps, rows, model = parts[0].shape
    out = (2, steps * len(parts), rows // 2, model)
    return pl.pallas_call(
        place_kernel,
        grid_spec=pltpu.PrefetchScalarGridSpec(
            num_scalar_prefetch=1,
            grid=(1,),
            in_specs=[pl.BlockSpec((steps, rows, model), lambda i, w: (0, 0, 0)) for _ in parts],
            out_specs=pl.BlockSpec(out, lambda i, w: (0, 0, 0, 0)),
        ),
        out_shape=jax.ShapeDtypeStruct(out, jnp.float32),
    )(where, *parts)


def local(
    section_tokens,
    enc_ln1,
    enc_qkv,
    enc_out,
    enc_ln2,
    enc_up,
    enc_down,
    set_latent,
    ray_queries,
    dec_query,
    dec_kv,
    dec_out,
    feature_grad,
):
    tokens = section_tokens[0, 0]
    width = tokens.shape[1]
    head_dim = width // HEADS
    local_width = enc_out.shape[1]
    sections = lax.axis_size("section")
    count = lax.axis_size("ray")
    groups = sections // HIGH
    line = groups // CORES
    latent = set_latent[0]
    queries = ray_queries[0]
    cotangent = feature_grad[0]
    rows, share = tokens.shape[0], dec_query.shape[0]
    f32, bf16 = jnp.float32, jnp.bfloat16
    here = lax.axis_index("section")
    core, place, high = here % CORES, here // CORES % line, here // groups

    normed = layer_norm(tokens, enc_ln1[0]).astype(bf16)
    seen = lax.all_gather(normed, "ray", axis=0, tiled=True)
    w_out = lax.all_gather(after(enc_out[0], normed), "ray", axis=0, tiled=True)

    steps = (0, 1, -1, 2)
    own = jnp.stack([queries, cotangent])
    own = after(own, normed)
    ring = {0: own, 1: moved(own, along=1), -1: moved(own, along=-1)}
    partner = {0: moved(own, core=1)}

    far_rows = moved(dec_out, high=1)
    wo = jnp.where(
        high == 0,
        jnp.concatenate([dec_out, far_rows], 0),
        jnp.concatenate([far_rows, dec_out], 0),
    )
    wo_line = jnp.concatenate(
        [wo, moved(wo, along=1), moved(wo, along=-1), moved(wo, along=2)], 0
    )

    q_cols = dec_query.reshape(share, HIGH, groups, head_dim).transpose(2, 0, 1, 3)
    kv_cols = dec_kv.reshape(share, 2, HIGH, groups, head_dim).transpose(3, 0, 2, 1, 4)
    cols = jnp.concatenate(
        [q_cols.reshape(groups, share, -1), kv_cols.reshape(groups, share, -1)], 2
    )
    cols = jnp.concatenate([cols] * HIGH, 0)
    w_heads = exchange(cols, "section").reshape(width, -1)
    wq = w_heads[:, : 2 * head_dim].T
    w_pairs = w_heads[:, 2 * head_dim :]
    own_pairs = jnp.dot(latent, w_pairs, preferred_element_type=f32).astype(bf16)
    pairs = gather_small(own_pairs, "ray").reshape(count * rows, -1)

    seen, ring[1], ring[-1], partner[0], own = lax.optimization_barrier(
        (seen, ring[1], ring[-1], partner[0], own, own_pairs, wo)
    )[:5]
    ring[2] = moved(own, along=2)
    partner[1], partner[-1] = moved(ring[1], core=1), moved(ring[-1], core=1)
    packed = jnp.dot(
        seen, enc_qkv[0].reshape(width, 3 * local_width), preferred_element_type=f32
    ).astype(bf16)
    packed, pairs, wo, wq = lax.optimization_barrier((packed, pairs, wo, wq))
    mixed = attend_heads(packed, head_dim)
    mixed = mixed.reshape(count, rows, -1)
    columns = exchange(mixed, "ray")

    pairs, partner[1], wo, wo_line = lax.optimization_barrier(
        (pairs, partner[1], wo, wo_line, mixed)
    )[:4]
    mixed_a, sums, proj = attend_rays(
        [ring[0], partner[0], ring[1], partner[1]], wq, wo, pairs, (), f32
    )
    columns, w_out, sums, ring[2] = lax.optimization_barrier((columns, w_out, sums, ring[2]))
    attn = jnp.einsum(
        "rtc,rcd->rtd", columns, w_out.reshape(count, -1, width), preferred_element_type=f32
    ).astype(bf16)
    attn_rows = jnp.sum(attn.astype(f32), 0)
    hidden = (tokens.astype(f32) + attn_rows).astype(bf16)
    normed_two = layer_norm(hidden, enc_ln2[0]).astype(bf16)
    seen_two = lax.all_gather(normed_two, "ray", axis=0, tiled=True)
    ring[2], wo_line = lax.optimization_barrier((ring[2], wo_line, normed_two))[:2]
    partner[2] = moved(ring[2], core=1)
    wo_other = moved(wo_line, core=1)
    mixed_b, sums, proj = attend_rays(
        [ring[-1], partner[-1], ring[2], partner[2]], wq, wo, pairs, (sums, proj), bf16
    )

    term = exchange(proj.reshape(count, -1, width), "ray")

    seen_two, term = lax.optimization_barrier((seen_two, term))
    upper = jax.nn.gelu(
        jnp.dot(seen_two, enc_up[0], preferred_element_type=f32), approximate=True
    ).astype(bf16)
    lower = jnp.dot(upper, enc_down[0], preferred_element_type=f32).astype(bf16)
    lower_rows = lax.psum_scatter(lower, "ray", scatter_dimension=0, tiled=True)

    term, sums, wo_line, wo_other = lax.optimization_barrier(
        (term, sums, wo_line, wo_other, lower)
    )[:4]
    term = jnp.sum(term.astype(f32), 0)
    term = term + moved(term, high=1)
    term = term + lax.ppermute(term, "dp", [(0, 1), (1, 0)])
    term, sums = lax.optimization_barrier((term.astype(bf16), sums))
    pair_sum = exchange(sums.reshape(count, rows, -1), "ray")
    term = gather_small(term, "ray").reshape(2 * head_dim, width)
    blocks = [mixed_a[0], mixed_a[1], mixed_a[2], mixed_a[3]]
    mixed_b = after(mixed_b, lower)
    blocks += [mixed_b[0], mixed_b[1], mixed_b[2], mixed_b[3]]
    back = {(k, c): blocks[2 * i + c] for i, k in enumerate(steps) for c in range(CORES)}
    mixed_t = {}
    for k in steps:
        for c in range(CORES):
            source = back[-k if k != 2 else 2, c]
            mixed_t[k, c] = moved(source, along=k, core=c) if k or c else source
    features = queries.astype(f32)
    for c, w_mix in ((0, wo_line), (1, wo_other)):
        side = jnp.concatenate([mixed_t[k, c] for k in steps], 0)
        features = features + lax.dot_general(side, w_mix, TN, preferred_element_type=f32)
    features = features.astype(bf16)

    half = term.shape[0] // 2
    grads = {0: term, 1: moved(term, along=1), -1: moved(term, along=-1)}
    grads[2] = jnp.concatenate(
        [moved(grads[1][:half], along=1), moved(grads[-1][half:], along=-1)], 0
    )
    grads = jnp.stack([grads[k] for k in steps])
    where = [(place - k) % line * CORES + (core ^ c) for c in range(CORES) for k in steps]

    pair_sum = jnp.sum(after(pair_sum, grads).astype(f32), 0).astype(bf16)
    latent_part = lax.dot_general(pair_sum, w_pairs, NT, preferred_element_type=f32).astype(bf16)
    latent_rows = exchange(latent_part.reshape(sections, -1, width), "section")
    latent_rows = jnp.sum(latent_rows.astype(f32), 0).astype(bf16)
    latent_grad = gather_small(latent_rows, "section").reshape(rows, width)
    other_grads = moved(grads, core=1)
    out_grad = placed([grads, other_grads], jnp.stack(where).astype(jnp.int32)).reshape(width, width)

    lower_rows = after(lower_rows, latent_part, features, out_grad)
    layer_out = (hidden.astype(f32) + lower_rows.astype(f32)).astype(bf16)
    handed = lax.ppermute(layer_out, "section", [(i, i + 1) for i in range(sections - 1)])
    finished = exchange(layer_out.T.reshape(sections, -1, rows), "section")[sections - 1].T
    return (handed[None, None], finished[None], features[None], latent_grad[None], out_grad)


def solution(mesh):
    return jax.shard_map(
        local,
        mesh=mesh,
        in_specs=(
            P("section", "dp", "ray", None),
            P("section", None),
            P("section", None, None, "ray"),
            P("section", "ray", None),
            P("section", None),
            P("section", None, "ray"),
            P("section", "ray", None),
            P("dp", "ray", None),
            P("dp", ("section", "ray"), None),
            P("section", None),
            P("section", None, None),
            P("section", None),
            P("dp", ("section", "ray"), None),
        ),
        out_specs=(
            P("section", "dp", "ray", None),
            P("dp", "ray", "section"),
            P("dp", ("section", "ray"), None),
            P("dp", "ray", None),
            P(),
        ),
        check_vma=False,
    )
```
